32 devices in a mesh: group: 2 (over y), ctx: 8 (over z, x), tp: 2 (over core).
Axes of the slice: x: 2, y: 2, z: 4, core: 2. Of those that a mesh axis runs over, the one named last changes fastest.
Arguments:
- queries: bfloat16 [2048, 4096], P(('group', 'ctx'), 'tp'), parts along dimension 0, may hold values from -1.796875 to 1.796875
- key_rows: bfloat16 [2048, 4096], P(('group', 'ctx'), 'tp'), parts along dimension 0, may hold values from -1.796875 to 1.796875
- value_rows: bfloat16 [2048, 4096], P(('group', 'ctx'), 'tp'), parts along dimension 0, may hold values from -6 to 6
- out_grad: bfloat16 [2048, 4096], P(('group', 'ctx', 'tp')), parts along dimension 0, may hold values from -0.119628906 to 0.119628906
- log_decay: float32 [2048, 32], P(('group', 'ctx'), 'tp'), parts along dimension 0, may hold values from -0.8 to 0
- doc_ids: int32 [32], P('group'), parts along dimension 0, may hold values from 0 to 3, never falling along the last dimension, each value on 1 to 8 neighbouring positions
Outputs:
- key_grad: bfloat16 [2048, 4096], P(('group', 'ctx'), 'tp'), parts along dimension 0
- value_grad: bfloat16 [2048, 4096], P(('group', 'ctx'), 'tp'), parts along dimension 0
The draws below stay inside these ranges and needn't reach their ends.
There are 2 independent parts, one for each index of `group`. The reference program is written for one: setup_inputs(seed, part) draws one part's arguments, and reference() takes and returns one part's arrays. A program takes and returns all parts, laid end to end along the dimension named above; each array names one. Nothing has to cross between parts.
Inputs may be any that keep to these rules, and one draw needn't show every extreme that they name: `doc_ids`: one entry per block of 64 positions; each document covers 1 to 8 consecutive blocks, one exactly 8; document numbers never fall.
All inputs are finite; a program needn't handle non-finite values.
Results may differ from the reference program's by a relative error of at most 0.0056.
Values may be sent and summed in bfloat16 or wider, within the bound.
A program may use at most 64 MiB of HBM per device.

```python
import math
import jax
import jax.numpy as jnp
import numpy as np
from jax import lax

H = 32
DH = 128
BLOCK = 64
DOCS = 4
ROWS = 128
SEQ = 1024
BLOCKS = 16


def draw_log_decay(key, part):
    streams = jax.random.split(jax.random.fold_in(key, 17), 6)
    fast_share = 0.5
    head_fast = jax.random.uniform(streams[0], (H,)) < fast_share
    fast_rate = jax.random.uniform(streams[1], (H,), minval=1.0 / 50.0, maxval=1.0 / 30.0)
    slow_rate = jax.random.uniform(streams[2], (H,), minval=0.1, maxval=0.8) / SEQ
    base_rate = jnp.where(head_fast, fast_rate, slow_rate)
    roughness = jnp.exp(jax.random.uniform(streams[3], (SEQ, H), minval=-0.69, maxval=0.69))
    bursting = jax.random.uniform(streams[4], (SEQ, H)) < 3.0 / SEQ
    dropped = jnp.log(jax.random.uniform(streams[5], (SEQ, H), minval=0.5, maxval=0.8))
    values_out = -base_rate[None, :] * roughness + jnp.where(bursting, dropped, 0.0)
    return values_out.astype(jnp.float32)


def level_of(own_key, extent, shards, least, top_value):
    gain = 1.0
    for dim, shards_of in shards:
        steps = jax.random.uniform(jax.random.fold_in(jax.random.fold_in(own_key, 6), dim), (shards_of,), jnp.float32, least / len(shards), top_value / len(shards))
        gain = gain * jnp.repeat(jnp.exp(steps), extent[dim] // shards_of).reshape((-1,) + (1,) * (len(extent) - 1 - dim))
    return gain


def split_up(number_of, total, limit, lean):
    weights = [(1 << 20) // math.isqrt(standing ** lean) + 1 for standing in range(2, number_of + 1)]
    rest, counts = total - limit - (number_of - 1), [1] * (number_of - 1)
    while rest > 0:
        candidates = [i for i in range(number_of - 1) if counts[i] < limit]
        pool, left = sum([weights[i] for i in candidates]), rest
        for i in candidates:
            extra = min(limit - counts[i], max(1, left * weights[i] // pool), rest)
            counts[i] = counts[i] + extra
            rest = rest - extra
    return np.array([limit] + counts)


def ragged(stream_key, count, total, limit, lean):
    if count == 2:
        one = jax.random.randint(stream_key, (), max(1, total - limit), min(limit, total - 1) + 1)
        return jnp.stack([one, total - one])
    tallies = jnp.asarray(split_up(count, total, limit, lean), jnp.int32)
    couples = (count - 1) // 2
    donor, taker = tallies[1:1 + 2 * couples:2], tallies[2:2 + 2 * couples:2]
    room = jnp.minimum(donor - 1, limit - taker)
    shifted = jax.random.randint(jax.random.fold_in(stream_key, 1), (couples,), 0, 1 << 20) % (room + 1)
    tallies = tallies.at[1:1 + 2 * couples:2].set(donor - shifted).at[2:2 + 2 * couples:2].set(taker + shifted)
    return tallies[jax.random.permutation(jax.random.fold_in(stream_key, 2), count)]


def scatter_about(stream_key, shape, deviation, reach, cuts=(), kind=jnp.bfloat16):
    result = deviation * jax.random.normal(stream_key, shape, jnp.float32)
    if cuts:
        result = result * level_of(stream_key, shape, cuts, -0.22, 0.18)
    return jnp.clip(result, -reach, reach).astype(kind)


def setup_inputs(seed: int = 0, part: int = 0) -> dict:
    keys = jax.random.split(jax.random.key(seed), 7)
    part_splits = jax.random.split(jax.random.fold_in(keys[6], part), 7)
    queries = scatter_about(part_splits[0], (SEQ, H * DH), 0.3, 1.796875, ((0, 8), (1, 2)))
    key_rows = scatter_about(part_splits[1], (SEQ, H * DH), 0.3, 1.796875, ((0, 8), (1, 2)))
    value_rows = scatter_about(part_splits[2], (SEQ, H * DH), 1.0, 6.0, ((0, 8), (1, 2)))
    out_grad = scatter_about(part_splits[3], (SEQ, H * DH), 0.02, 0.119628906, ((0, 16),))
    log_decay = draw_log_decay(jax.random.fold_in(jax.random.fold_in(keys[6], part), 71), part)
    doc_ids = jnp.searchsorted(jnp.cumsum(ragged(part_splits[5], DOCS, BLOCKS, BLOCKS // 2, 0)), jnp.arange(BLOCKS), side="right").astype(jnp.int32)
    return dict(queries=queries, key_rows=key_rows, value_rows=value_rows, out_grad=out_grad, log_decay=log_decay, doc_ids=doc_ids)


def product(pattern, first_op, second_op, promote):
    if promote:
        first_op = lax.optimization_barrier(first_op)
        second_op = lax.optimization_barrier(second_op)
        return jnp.einsum(pattern, first_op.astype(jnp.float32), second_op.astype(jnp.float32))
    return jnp.einsum(pattern, first_op, second_op, preferred_element_type=jnp.float32)


def span_terms(queries, key_rows, value_rows, grad_rows, log_decay, doc_rows, prev_doc, promote):
    row_count, head_count = log_decay.shape
    head_size = queries.shape[1] // head_count
    query_heads = queries.reshape(row_count, head_count, head_size)
    key_heads = key_rows.reshape(row_count, head_count, head_size)
    value_heads = value_rows.reshape(row_count, head_count, head_size)
    grad_heads = grad_rows.reshape(row_count, head_count, head_size)
    cumulative = jnp.cumsum(log_decay.T.astype(jnp.float32), axis=1)
    spread = cumulative[:, :, None] - cumulative[:, None, :]
    position = jnp.arange(row_count)
    allowed = (position[:, None] >= position[None, :]) & (doc_rows[:, None] == doc_rows[None, :])
    weight = jnp.where(allowed[None], jnp.exp(jnp.minimum(spread, 0.0)), 0.0)
    grad_value = product("thd,shd->hts", grad_heads, value_heads, promote)
    query_key = product("thd,shd->hts", query_heads, key_heads, promote)
    mixed_gv = (weight * grad_value).astype(jnp.bfloat16)
    mixed_qk = (weight * query_key).astype(jnp.bfloat16)
    key_inner = product("hts,thd->shd", mixed_gv, query_heads, promote)
    value_inner = product("hts,thd->shd", mixed_qk, grad_heads, promote)
    first_doc = doc_rows[0]
    last_doc = doc_rows[-1]
    linked = (prev_doc == first_doc).astype(jnp.float32)
    lead_mask = (doc_rows == first_doc).astype(jnp.float32)
    scaling = jnp.exp(cumulative).T * lead_mask[:, None]
    scaled = (query_heads.astype(jnp.float32) * scaling[:, :, None]).astype(jnp.bfloat16)
    state = product("thi,thj->hij", scaled, grad_heads, promote) * linked
    through = linked * (first_doc == last_doc).astype(jnp.float32)
    factor = through * jnp.exp(cumulative[:, -1])
    tail_mask = (doc_rows == last_doc).astype(jnp.float32)
    weight_in = jnp.exp(cumulative[:, -1:] - cumulative) * tail_mask[None, :]
    return key_inner, value_inner, state, factor, weight_in


def apply_state(incoming, key_rows, value_rows, weight_in, key_inner, value_inner, promote):
    row_count = key_rows.shape[0]
    head_count, head_size = incoming.shape[0], incoming.shape[1]
    key_heads = key_rows.reshape(row_count, head_count, head_size)
    value_heads = value_rows.reshape(row_count, head_count, head_size)
    rounded = incoming.astype(jnp.bfloat16)
    to_keys = product("hij,shj->shi", rounded, value_heads, promote)
    to_values = product("hij,shi->shj", rounded, key_heads, promote)
    scaling = weight_in.T[:, :, None]
    key_grad = (key_inner + scaling * to_keys).astype(jnp.bfloat16).reshape(row_count, head_count * head_size)
    value_grad = (value_inner + scaling * to_values).astype(jnp.bfloat16).reshape(row_count, head_count * head_size)
    return key_grad, value_grad


def reference(queries, key_rows, value_rows, out_grad, log_decay, doc_ids):
    span_count = SEQ // ROWS
    feature_count = H * DH
    query_spans = queries.reshape(span_count, ROWS, feature_count)
    key_spans = key_rows.reshape(span_count, ROWS, feature_count)
    value_spans = value_rows.reshape(span_count, ROWS, feature_count)
    grad_spans = out_grad.reshape(span_count, ROWS, feature_count)
    decay_spans = log_decay.reshape(span_count, ROWS, H)
    doc_spans = jnp.repeat(doc_ids, BLOCK).reshape(span_count, ROWS).astype(jnp.int32)
    prev_docs = jnp.concatenate([jnp.full((1,), -1, jnp.int32), doc_spans[:-1, -1].astype(jnp.int32)])

    def backward_span(incoming, pieces):
        query_c, key_c, value_c, grad_c, decay_c, doc_c, prev_c = pieces
        key_inner, value_inner, state, factor, weight_in = span_terms(query_c, key_c, value_c, grad_c, decay_c, doc_c, prev_c, True)
        key_grad, value_grad = apply_state(incoming, key_c, value_c, weight_in, key_inner, value_inner, True)
        return state + factor[:, None, None] * incoming, (key_grad, value_grad)

    start_state = jnp.zeros((H, DH, DH), jnp.float32)
    _, (key_grad, value_grad) = lax.scan(backward_span, start_state, (query_spans, key_spans, value_spans, grad_spans, decay_spans, doc_spans, prev_docs), reverse=True)
    return key_grad.reshape(SEQ, feature_count), value_grad.reshape(SEQ, feature_count)
```

```python
import functools

import jax
import jax.numpy as jnp
from jax import lax
from jax.experimental import pallas as pl
from jax.experimental.pallas import tpu as pltpu
from jax.sharding import PartitionSpec as P

BLOCK = 64
DH = 128
PIECES = 2
MESH = pl.DeviceIdType.MESH


def dot(a, b, dims):
    return lax.dot_general(a, b, (dims, ((), ())), preferred_element_type=jnp.float32)


NN = ((1,), (0,))
NT = ((1,), (1,))


def kernel(ctx_count, heads, shared, docs, decay, q_hbm, k_hbm, v_hbm, og_hbm, dk, dv,
           q, k, v, g, turned, cum, lead_row, tail_row, factor, factor_other, mine, given, other, sent, later,
           handed, back, held, key_inner, value_inner, allowed,
           load_sem, swap_sem, fac_sem, pair_send, pair_recv, chain_send, chain_recv, back_send, back_recv):
    rows = q.shape[0]
    half = og_hbm.shape[0]
    width = q.shape[1]
    owned = (heads - shared) // 2
    steps = owned + shared
    group, ctx, tp = lax.axis_index("group"), lax.axis_index("ctx"), lax.axis_index("tp")
    odd = lax.rem(ctx, 2)
    even = odd == 0
    pair = (group, ctx + 1 - 2 * odd, tp)
    core = (group, ctx, 1 - tp)
    before = (group, ctx - 2, tp)
    after = (group, ctx + 2, tp)
    has_before = ctx >= 2
    has_after = ctx < ctx_count - 2
    own_base, pair_base = odd * owned, (1 - odd) * owned

    barrier = pltpu.get_barrier_semaphore()
    for peer in (pair, core):
        pl.semaphore_signal(barrier, inc=1, device_id=peer, device_id_type=MESH)

    @pl.when(has_before)
    def _():
        pl.semaphore_signal(barrier, inc=1, device_id=before, device_id_type=MESH)

    @pl.when(has_after)
    def _():
        pl.semaphore_signal(barrier, inc=1, device_id=after, device_id_type=MESH)

    own_rows = pl.ds(pl.multiple_of(tp * half, half), half)
    loads = [pltpu.make_async_copy(src, dst, load_sem.at[i])
             for i, (src, dst) in enumerate((
                 (q_hbm, q),
                 (og_hbm.at[:, pl.ds(pl.multiple_of(tp * width, width), width)], g.at[own_rows, :]),
                 (k_hbm, k), (v_hbm, v)))]
    for copy in loads:
        copy.start()

    blocks = rows // BLOCK
    doc_list = [docs[ctx * blocks + b] for b in range(blocks)]
    first, last = doc_list[0], doc_list[-1]
    prev = docs[jnp.maximum(ctx * blocks - 1, 0)]
    linked = jnp.where((ctx > 0) & (prev == first), 1.0, 0.0).astype(jnp.float32)
    through = jnp.where(first == last, linked, 0.0).astype(jnp.float32)

    def doc_of(position):
        doc = jnp.full(position.shape, first, jnp.int32)
        for b in range(1, blocks):
            doc = jnp.where(position >= b * BLOCK, doc_list[b], doc)
        return doc

    lane = lax.broadcasted_iota(jnp.int32, (heads, rows), 1)
    total = decay[...]
    step = 1
    while step < rows:
        total = total + jnp.where(lane >= step, pltpu.roll(total, step, 1), 0.0)
        step *= 2
    lane_doc = doc_of(lane)
    ending = jnp.broadcast_to(total[:, rows - 1:rows], (heads, rows))
    cum[...] = total
    lead_row[...] = jnp.where(lane_doc == first, jnp.exp(total) * linked, 0.0)
    tail_row[...] = jnp.where(lane_doc == last, jnp.exp(ending - total), 0.0)
    factor[...] = jnp.exp(ending) * through
    key_at = lax.broadcasted_iota(jnp.int32, (rows, rows), 0)
    query_at = lax.broadcasted_iota(jnp.int32, (rows, rows), 1)
    allowed[...] = jnp.where(
        (query_at >= key_at) & (doc_of(query_at) == doc_of(key_at)), 1.0, 0.0)

    def columns(h):
        return pl.ds(pl.multiple_of(h * DH, DH), DH)

    loads[0].wait()

    def turn_step(i, carry):
        for j in range(2):
            h = 2 * i + j
            flipped = q[:, columns(h)].astype(jnp.float32).T
            turned[h] = (flipped * lead_row[pl.ds(h, 1), :]).astype(jnp.bfloat16)
        return carry

    lax.fori_loop(0, heads // 2, turn_step, 0)

    pl.semaphore_wait(barrier, 2 + has_before.astype(jnp.int32) + has_after.astype(jnp.int32))

    swaps = []
    for n, (start, count) in enumerate(((pair_base, owned), (2 * owned, shared), (own_base, owned))):
        theirs = pl.ds(pl.multiple_of((1 - tp) * width + start * DH, DH), count * DH)
        swaps.append(pltpu.make_async_remote_copy(
            src_ref=og_hbm.at[:, theirs],
            dst_ref=g.at[own_rows, pl.ds(pl.multiple_of(start * DH, DH), count * DH)],
            send_sem=swap_sem.at[0, n], recv_sem=swap_sem.at[1, n],
            device_id=core, device_id_type=MESH))
    for swap in swaps:
        swap.start()
    fac_copy = pltpu.make_async_remote_copy(
        src_ref=factor, dst_ref=factor_other, send_sem=fac_sem.at[0], recv_sem=fac_sem.at[1],
        device_id=pair, device_id_type=MESH)
    fac_copy.start()

    piece_rows = DH // PIECES

    def piece(j):
        return pl.ds(j * piece_rows, piece_rows)

    def pair_copy(i, j):
        return pltpu.make_async_remote_copy(
            src_ref=given.at[i, piece(j)], dst_ref=other.at[i, piece(j)],
            send_sem=pair_send.at[i, j], recv_sem=pair_recv.at[i, j],
            device_id=pair, device_id_type=MESH)

    def chain_copy(i, j):
        return pltpu.make_async_remote_copy(
            src_ref=sent.at[i, piece(j)], dst_ref=later.at[i, piece(j)],
            send_sem=chain_send.at[i, j], recv_sem=chain_recv.at[i, j],
            device_id=before, device_id_type=MESH)

    def back_copy(i, j):
        return pltpu.make_async_remote_copy(
            src_ref=handed.at[i, piece(j)], dst_ref=back.at[i, piece(j)],
            send_sem=back_send.at[i, j], recv_sem=back_recv.at[i, j],
            device_id=pair, device_id_type=MESH)

    def state_of(h):
        return dot(turned[h], g[:, columns(h)], NN)

    loads[1].wait()

    def give_step(i, carry):
        for j in range(2):
            given[2 * i + j] = state_of(pair_base + 2 * i + j).astype(given.dtype)
        for j in range(2):
            for p in range(PIECES):
                pair_copy(2 * i + j, p).start()
        return carry

    def share_step(i, carry):
        for j in range(2):
            at = owned + 2 * i + j
            state = state_of(owned + at)
            mine[at] = state
            given[at] = state.astype(given.dtype)
        for j in range(2):
            for p in range(PIECES):
                pair_copy(owned + 2 * i + j, p).start()
        return carry

    def keep_step(i, carry):
        for j in range(2):
            mine[2 * i + j] = state_of(own_base + 2 * i + j)
        return carry

    swaps[0].wait()
    lax.fori_loop(0, owned // 2, give_step, 0)
    swaps[1].wait()
    lax.fori_loop(0, shared // 2, share_step, 0)
    swaps[2].wait()
    lax.fori_loop(0, owned // 2, keep_step, 0)
    loads[2].wait()
    loads[3].wait()

    def inner(h):
        cols = columns(h)
        qh, gh = q[:, cols], g[:, cols]
        along = jnp.broadcast_to(cum[pl.ds(h, 1), :], (rows, rows))
        weight = allowed[...] * jnp.exp(jnp.minimum(along - along.T, 0.0))
        mixed_gv = (weight * dot(v[:, cols], gh, NT)).astype(jnp.bfloat16)
        mixed_qk = (weight * dot(k[:, cols], qh, NT)).astype(jnp.bfloat16)
        key_inner[:, cols] = dot(mixed_gv, qh, NN)
        value_inner[:, cols] = dot(mixed_qk, gh, NN)

    def apply(h, state_in):
        cols = columns(h)
        scale = jnp.broadcast_to(tail_row[pl.ds(h, 1), :], (rows, rows)).T
        dk[:, cols] = (key_inner[:, cols] + scale * dot(v[:, cols], state_in, NT)).astype(dk.dtype)
        dv[:, cols] = (value_inner[:, cols] + scale * dot(k[:, cols], state_in, NN)).astype(dv.dtype)

    def early_step(i, carry):
        inner(2 * i)
        inner(2 * i + 1)
        return carry

    early = heads - steps
    lax.fori_loop(0, jnp.where(has_after, heads // 2, early // 2), early_step, 0)
    fac_copy.wait()

    def chain_piece(i, h, j, gives_back):
        at = piece(j)
        pair_copy(i, j).wait_recv()
        own_state, pair_state = mine[i, at, :], other[i, at, :].astype(jnp.float32)
        own_factor, pair_factor = factor[pl.ds(h, 1), :], factor_other[pl.ds(h, 1), :]
        state_even = jnp.where(even, own_state, pair_state)
        state_odd = jnp.where(even, pair_state, own_state)
        factor_even = jnp.where(even, own_factor, pair_factor)
        factor_odd = jnp.where(even, pair_factor, own_factor)
        joined = state_even + factor_even * state_odd

        @pl.when(has_after)
        def _():
            chain_copy(i, j).wait_recv()

        incoming = jnp.where(has_after, later[i, at, :].astype(jnp.float32), 0.0)

        @pl.when(has_before)
        def _():
            sent[i, at, :] = (joined + (factor_even * factor_odd) * incoming).astype(sent.dtype)
            chain_copy(i, j).start()

        into_even = (state_odd + factor_odd * incoming).astype(jnp.bfloat16)
        into_odd = incoming.astype(jnp.bfloat16)
        if gives_back:
            handed[i, at, :] = jnp.where(even, into_odd, into_even)
            back_copy(i, j).start()
        held[i, at, :] = jnp.where(even, into_even, into_odd)

    def late_inner(i):
        @pl.when(jnp.logical_not(has_after))
        def _():
            inner(early + i)

    def owned_step(i, carry):
        for j in range(PIECES):
            chain_piece(i, own_base + i, j, True)
        late_inner(i)
        return carry

    def shared_step(i, carry):
        for j in range(PIECES):
            chain_piece(i, owned + i, j, False)
        late_inner(i)
        return carry

    lax.fori_loop(0, owned, owned_step, 0)
    lax.fori_loop(owned, steps, shared_step, 0)

    def own_step(i, carry):
        for j in range(2):
            apply(own_base + 2 * i + j, held[2 * i + j])
        return carry

    def both_step(i, carry):
        for j in range(2):
            at = owned + 2 * i + j
            apply(owned + at, held[at])
        return carry

    lax.fori_loop(0, owned // 2, own_step, 0)
    lax.fori_loop(0, shared // 2, both_step, 0)

    def last_step(i, carry):
        for j in range(PIECES):
            back_copy(i, j).wait_recv()
        apply(pair_base + i, back[i])
        return carry

    lax.fori_loop(0, owned, last_step, 0)

    def drain(i, carry):
        for j in range(PIECES):
            pair_copy(i, j).wait_send()

            @pl.when(has_before)
            def _():
                chain_copy(i, j).wait_send()

            @pl.when(i < owned)
            def _():
                back_copy(i, j).wait_send()

        return carry

    lax.fori_loop(0, steps, drain, 0)


def handover(a_in, b_in, a_out, b_out, sem):
    pieces = sem.shape[1]
    size = a_in.shape[0] // pieces
    moves = [pltpu.make_async_copy(src.at[pl.ds(size * i, size), :], dst.at[pl.ds(size * i, size), :], sem.at[n, i])
             for i in range(pieces) for n, (src, dst) in enumerate(((a_in, a_out), (b_in, b_out)))]
    for move in moves:
        move.start()
    for move in moves:
        move.wait()


def solution(mesh):
    ctx_count = mesh.shape["ctx"]
    wire = jnp.bfloat16 if ctx_count <= 8 else jnp.float32

    def per_device(queries, key_rows, value_rows, out_grad, log_decay, doc_ids):
        rows, features = queries.shape
        heads = log_decay.shape[1]
        shared = heads // 4
        owned = (heads - shared) // 2
        steps = owned + shared
        anywhere = pl.BlockSpec(memory_space=pl.ANY)
        in_vmem = pl.BlockSpec(memory_space=pltpu.VMEM)
        wide = pltpu.VMEM((rows, features), jnp.bfloat16)
        small = pltpu.VMEM((heads, rows), jnp.float32)
        states = pltpu.VMEM((steps, DH, DH), wire)
        total = pltpu.VMEM((rows, features), jnp.float32)
        many = pltpu.SemaphoreType.DMA((steps, PIECES))
        shape = jax.ShapeDtypeStruct((rows, features), jnp.bfloat16)
        inside = pltpu.MemorySpace.VMEM((rows, features), jnp.bfloat16)
        key_grad, value_grad = pl.pallas_call(
            functools.partial(kernel, ctx_count, heads, shared),
            out_shape=(inside, inside),
            in_specs=[pl.BlockSpec(memory_space=pltpu.SMEM), in_vmem] + [anywhere] * 4,
            out_specs=(in_vmem, in_vmem),
            scratch_shapes=[wide] * 4 + [pltpu.VMEM((heads, DH, rows), jnp.bfloat16)] + [small] * 5 + [
                pltpu.VMEM((steps, DH, DH), jnp.float32)] + [states] * 4 + [
                pltpu.VMEM((owned, DH, DH), jnp.bfloat16)] * 2 + [
                pltpu.VMEM((steps, DH, DH), jnp.bfloat16)] + [total] * 2 + [
                pltpu.VMEM((rows, rows), jnp.float32)] + [
                pltpu.SemaphoreType.DMA((4,)), pltpu.SemaphoreType.DMA((2, 3)), pltpu.SemaphoreType.DMA((2,)),
                many, many, many, many, many, many],
            compiler_params=pltpu.CompilerParams(
                collective_id=0, has_side_effects=True, vmem_limit_bytes=24 << 20),
        )(doc_ids, log_decay.T, queries, key_rows, value_rows, out_grad)
        return tuple(pl.pallas_call(
            handover,
            out_shape=(shape, shape),
            in_specs=[in_vmem] * 2,
            out_specs=(anywhere, anywhere),
            scratch_shapes=[pltpu.SemaphoreType.DMA((2, 4))],
            compiler_params=pltpu.CompilerParams(vmem_limit_bytes=16 << 20),
        )(key_grad, value_grad))

    placed = (
        P(("group", "ctx"), "tp"),
        P(("group", "ctx"), "tp"),
        P(("group", "ctx"), "tp"),
        P(("group", "ctx", "tp"), None),
        P(("group", "ctx"), "tp"),
        P("group"),
    )
    return jax.shard_map(
        per_device,
        mesh=mesh,
        in_specs=placed,
        out_specs=(P(("group", "ctx"), "tp"), P(("group", "ctx"), "tp")),
        check_vma=False,
    )
```

```python
import functools

import jax
import jax.numpy as jnp
from jax import lax
from jax.experimental import pallas as pl
from jax.experimental.pallas import tpu as pltpu
from jax.sharding import PartitionSpec as P

BLOCK = 64
DH = 128
PIECES = 2
MESH = pl.DeviceIdType.MESH


def dot(a, b, dims):
    return lax.dot_general(a, b, (dims, ((), ())), preferred_element_type=jnp.float32)


NN = ((1,), (0,))
NT = ((1,), (1,))


def kernel(ctx_count, heads, shared, docs, decay, q_hbm, k_hbm, v_hbm, og_hbm, dk, dv,
           q, k, v, g, turned, cum, lead_row, tail_row, factor, factor_other, mine, given, other, sent, later,
           handed, back, held, key_inner, value_inner, allowed,
           load_sem, swap_sem, fac_sem, pair_send, pair_recv, chain_send, chain_recv, back_send, back_recv):
    rows = q.shape[0]
    half = og_hbm.shape[0]
    width = q.shape[1]
    owned = (heads - shared) // 2
    steps = owned + shared
    group, ctx, tp = lax.axis_index("group"), lax.axis_index("ctx"), lax.axis_index("tp")
    odd = lax.rem(ctx, 2)
    even = odd == 0
    pair = (group, ctx + 1 - 2 * odd, tp)
    core = (group, ctx, 1 - tp)
    before = (group, ctx - 2, tp)
    after = (group, ctx + 2, tp)
    has_before = ctx >= 2
    has_after = ctx < ctx_count - 2
    own_base, pair_base = odd * owned, (1 - odd) * owned

    barrier = pltpu.get_barrier_semaphore()
    for peer in (pair, core):
        pl.semaphore_signal(barrier, inc=1, device_id=peer, device_id_type=MESH)

    @pl.when(has_before)
    def _():
        pl.semaphore_signal(barrier, inc=1, device_id=before, device_id_type=MESH)

    @pl.when(has_after)
    def _():
        pl.semaphore_signal(barrier, inc=1, device_id=after, device_id_type=MESH)

    own_rows = pl.ds(pl.multiple_of(tp * half, half), half)
    loads = [pltpu.make_async_copy(src, dst, load_sem.at[i])
             for i, (src, dst) in enumerate((
                 (q_hbm, q),
                 (og_hbm.at[:, pl.ds(pl.multiple_of(tp * width, width), width)], g.at[own_rows, :]),
                 (k_hbm, k), (v_hbm, v)))]
    for copy in loads:
        copy.start()

    blocks = rows // BLOCK
    doc_list = [docs[ctx * blocks + b] for b in range(blocks)]
    first, last = doc_list[0], doc_list[-1]
    prev = docs[jnp.maximum(ctx * blocks - 1, 0)]
    linked = jnp.where((ctx > 0) & (prev == first), 1.0, 0.0).astype(jnp.float32)
    through = jnp.where(first == last, linked, 0.0).astype(jnp.float32)

    def doc_of(position):
        doc = jnp.full(position.shape, first, jnp.int32)
        for b in range(1, blocks):
            doc = jnp.where(position >= b * BLOCK, doc_list[b], doc)
        return doc

    lane = lax.broadcasted_iota(jnp.int32, (heads, rows), 1)
    total = decay[...]
    step = 1
    while step < rows:
        total = total + jnp.where(lane >= step, pltpu.roll(total, step, 1), 0.0)
        step *= 2
    lane_doc = doc_of(lane)
    ending = jnp.broadcast_to(total[:, rows - 1:rows], (heads, rows))
    cum[...] = total
    lead_row[...] = jnp.where(lane_doc == first, jnp.exp(total) * linked, 0.0)
    tail_row[...] = jnp.where(lane_doc == last, jnp.exp(ending - total), 0.0)
    factor[...] = jnp.exp(ending) * through
    key_at = lax.broadcasted_iota(jnp.int32, (rows, rows), 0)
    query_at = lax.broadcasted_iota(jnp.int32, (rows, rows), 1)
    allowed[...] = jnp.where(
        (query_at >= key_at) & (doc_of(query_at) == doc_of(key_at)), 1.0, 0.0)

    def columns(h):
        return pl.ds(pl.multiple_of(h * DH, DH), DH)

    loads[0].wait()

    def turn_step(i, carry):
        for j in range(2):
            h = 2 * i + j
            flipped = q[:, columns(h)].astype(jnp.float32).T
            turned[h] = (flipped * lead_row[pl.ds(h, 1), :]).astype(jnp.bfloat16)
        return carry

    lax.fori_loop(0, heads // 2, turn_step, 0)

    pl.semaphore_wait(barrier, 2 + has_before.astype(jnp.int32) + has_after.astype(jnp.int32))

    swaps = []
    for n, (start, count) in enumerate(((pair_base, owned), (2 * owned, shared), (own_base, owned))):
        theirs = pl.ds(pl.multiple_of((1 - tp) * width + start * DH, DH), count * DH)
        swaps.append(pltpu.make_async_remote_copy(
            src_ref=og_hbm.at[:, theirs],
            dst_ref=g.at[own_rows, pl.ds(pl.multiple_of(start * DH, DH), count * DH)],
            send_sem=swap_sem.at[0, n], recv_sem=swap_sem.at[1, n],
            device_id=core, device_id_type=MESH))
    for swap in swaps:
        swap.start()
    fac_copy = pltpu.make_async_remote_copy(
        src_ref=factor, dst_ref=factor_other, send_sem=fac_sem.at[0], recv_sem=fac_sem.at[1],
        device_id=pair, device_id_type=MESH)
    fac_copy.start()

    piece_rows = DH // PIECES

    def piece(j):
        return pl.ds(j * piece_rows, piece_rows)

    def pair_copy(i, j):
        return pltpu.make_async_remote_copy(
            src_ref=given.at[i, piece(j)], dst_ref=other.at[i, piece(j)],
            send_sem=pair_send.at[i, j], recv_sem=pair_recv.at[i, j],
            device_id=pair, device_id_type=MESH)

    def chain_copy(i, j):
        return pltpu.make_async_remote_copy(
            src_ref=sent.at[i, piece(j)], dst_ref=later.at[i, piece(j)],
            send_sem=chain_send.at[i, j], recv_sem=chain_recv.at[i, j],
            device_id=before, device_id_type=MESH)

    def back_copy(i, j):
        return pltpu.make_async_remote_copy(
            src_ref=handed.at[i, piece(j)], dst_ref=back.at[i, piece(j)],
            send_sem=back_send.at[i, j], recv_sem=back_recv.at[i, j],
            device_id=pair, device_id_type=MESH)

    def state_of(h):
        return dot(turned[h], g[:, columns(h)], NN)

    loads[1].wait()

    def give_step(i, carry):
        for j in range(2):
            given[2 * i + j] = state_of(pair_base + 2 * i + j).astype(given.dtype)
        for j in range(2):
            for p in range(PIECES):
                pair_copy(2 * i + j, p).start()
        return carry

    def share_step(i, carry):
        for j in range(2):
            at = owned + 2 * i + j
            state = state_of(owned + at)
            mine[at] = state
            given[at] = state.astype(given.dtype)
        for j in range(2):
            for p in range(PIECES):
                pair_copy(owned + 2 * i + j, p).start()
        return carry

    def keep_step(i, carry):
        for j in range(2):
            mine[2 * i + j] = state_of(own_base + 2 * i + j)
        return carry

    swaps[0].wait()
    lax.fori_loop(0, owned // 2, give_step, 0)
    swaps[1].wait()
    lax.fori_loop(0, shared // 2, share_step, 0)
    swaps[2].wait()
    lax.fori_loop(0, owned // 2, keep_step, 0)
    loads[2].wait()
    loads[3].wait()

    def inner(h):
        cols = columns(h)
        qh, gh = q[:, cols], g[:, cols]
        along = jnp.broadcast_to(cum[pl.ds(h, 1), :], (rows, rows))
        weight = allowed[...] * jnp.exp(jnp.minimum(along - along.T, 0.0))
        mixed_gv = (weight * dot(v[:, cols], gh, NT)).astype(jnp.bfloat16)
        mixed_qk = (weight * dot(k[:, cols], qh, NT)).astype(jnp.bfloat16)
        key_inner[:, cols] = dot(mixed_gv, qh, NN)
        value_inner[:, cols] = dot(mixed_qk, gh, NN)

    def apply(h, state_in):
        cols = columns(h)
        scale = jnp.broadcast_to(tail_row[pl.ds(h, 1), :], (rows, rows)).T
        dk[:, cols] = (key_inner[:, cols] + scale * dot(v[:, cols], state_in, NT)).astype(dk.dtype)
        dv[:, cols] = (value_inner[:, cols] + scale * dot(k[:, cols], state_in, NN)).astype(dv.dtype)

    def early_step(i, carry):
        inner(2 * i)
        inner(2 * i + 1)
        return carry

    early = heads - steps
    lax.fori_loop(0, jnp.where(has_after, heads // 2, early // 2), early_step, 0)
    fac_copy.wait()

    def chain_piece(i, h, j, gives_back):
        at = piece(j)
        pair_copy(i, j).wait_recv()
        own_state, pair_state = mine[i, at, :], other[i, at, :].astype(jnp.float32)
        own_factor, pair_factor = factor[pl.ds(h, 1), :], factor_other[pl.ds(h, 1), :]
        state_even = jnp.where(even, own_state, pair_state)
        state_odd = jnp.where(even, pair_state, own_state)
        factor_even = jnp.where(even, own_factor, pair_factor)
        factor_odd = jnp.where(even, pair_factor, own_factor)
        joined = state_even + factor_even * state_odd

        @pl.when(has_after)
        def _():
            chain_copy(i, j).wait_recv()

        incoming = jnp.where(has_after, later[i, at, :].astype(jnp.float32), 0.0)

        @pl.when(has_before)
        def _():
            sent[i, at, :] = (joined + (factor_even * factor_odd) * incoming).astype(sent.dtype)
            chain_copy(i, j).start()

        into_even = (state_odd + factor_odd * incoming).astype(jnp.bfloat16)
        into_odd = incoming.astype(jnp.bfloat16)
        if gives_back:
            handed[i, at, :] = jnp.where(even, into_odd, into_even)
            back_copy(i, j).start()
        held[i, at, :] = jnp.where(even, into_even, into_odd)

    def late_inner(i):
        @pl.when(jnp.logical_not(has_after))
        def _():
            inner(early + i)

    def owned_step(i, carry):
        for j in range(PIECES):
            chain_piece(i, own_base + i, j, True)
        late_inner(i)
        return carry

    def shared_step(i, carry):
        for j in range(PIECES):
            chain_piece(i, owned + i, j, False)
        late_inner(i)
        return carry

    lax.fori_loop(0, owned, owned_step, 0)
    lax.fori_loop(owned, steps, shared_step, 0)

    def own_step(i, carry):
        for j in range(2):
            apply(own_base + 2 * i + j, held[2 * i + j])
        return carry

    def both_step(i, carry):
        for j in range(2):
            at = owned + 2 * i + j
            apply(owned + at, held[at])
        return carry

    lax.fori_loop(0, owned // 2, own_step, 0)
    lax.fori_loop(0, shared // 2, both_step, 0)

    def last_step(i, carry):
        for j in range(PIECES):
            back_copy(i, j).wait_recv()
        apply(pair_base + i, back[i])
        return carry

    lax.fori_loop(0, owned, last_step, 0)

    def drain(i, carry):
        for j in range(PIECES):
            pair_copy(i, j).wait_send()

            @pl.when(has_before)
            def _():
                chain_copy(i, j).wait_send()

            @pl.when(i < owned)
            def _():
                back_copy(i, j).wait_send()

        return carry

    lax.fori_loop(0, steps, drain, 0)


def handover(a_in, b_in, a_out, b_out, sem):
    pieces = sem.shape[1]
    size = a_in.shape[0] // pieces
    moves = [pltpu.make_async_copy(src.at[pl.ds(size * i, size), :], dst.at[pl.ds(size * i, size), :], sem.at[n, i])
             for i in range(pieces) for n, (src, dst) in enumerate(((a_in, a_out), (b_in, b_out)))]
    for move in moves:
        move.start()
    for move in moves:
        move.wait()


def solution(mesh):
    ctx_count = mesh.shape["ctx"]
    wire = jnp.bfloat16 if ctx_count <= 8 else jnp.float32

    def per_device(queries, key_rows, value_rows, out_grad, log_decay, doc_ids):
        rows, features = queries.shape
        heads = log_decay.shape[1]
        shared = heads // 4
        owned = (heads - shared) // 2
        steps = owned + shared
        anywhere = pl.BlockSpec(memory_space=pl.ANY)
        in_vmem = pl.BlockSpec(memory_space=pltpu.VMEM)
        wide = pltpu.VMEM((rows, features), jnp.bfloat16)
        small = pltpu.VMEM((heads, rows), jnp.float32)
        states = pltpu.VMEM((steps, DH, DH), wire)
        total = pltpu.VMEM((rows, features), jnp.float32)
        many = pltpu.SemaphoreType.DMA((steps, PIECES))
        shape = jax.ShapeDtypeStruct((rows, features), jnp.bfloat16)
        inside = pltpu.MemorySpace.VMEM((rows, features), jnp.bfloat16)
        key_grad, value_grad = pl.pallas_call(
            functools.partial(kernel, ctx_count, heads, shared),
            out_shape=(inside, inside),
            in_specs=[pl.BlockSpec(memory_space=pltpu.SMEM), in_vmem] + [anywhere] * 4,
            out_specs=(in_vmem, in_vmem),
            scratch_shapes=[wide] * 4 + [pltpu.VMEM((heads, DH, rows), jnp.bfloat16)] + [small] * 5 + [
                pltpu.VMEM((steps, DH, DH), jnp.float32)] + [states] * 4 + [
                pltpu.VMEM((owned, DH, DH), jnp.bfloat16)] * 2 + [
                pltpu.VMEM((steps, DH, DH), jnp.bfloat16)] + [total] * 2 + [
                pltpu.VMEM((rows, rows), jnp.float32)] + [
                pltpu.SemaphoreType.DMA((4,)), pltpu.SemaphoreType.DMA((2, 3)), pltpu.SemaphoreType.DMA((2,)),
                many, many, many, many, many, many],
            compiler_params=pltpu.CompilerParams(
                collective_id=0, has_side_effects=True, vmem_limit_bytes=62 << 20),
        )(doc_ids, log_decay.T, queries, key_rows, value_rows, out_grad)
        return tuple(pl.pallas_call(
            handover,
            out_shape=(shape, shape),
            in_specs=[in_vmem] * 2,
            out_specs=(anywhere, anywhere),
            scratch_shapes=[pltpu.SemaphoreType.DMA((2, 4))],
            compiler_params=pltpu.CompilerParams(vmem_limit_bytes=16 << 20),
        )(key_grad, value_grad))

    placed = (
        P(("group", "ctx"), "tp"),
        P(("group", "ctx"), "tp"),
        P(("group", "ctx"), "tp"),
        P(("group", "ctx", "tp"), None),
        P(("group", "ctx"), "tp"),
        P("group"),
    )
    return jax.shard_map(
        per_device,
        mesh=mesh,
        in_specs=placed,
        out_specs=(P(("group", "ctx"), "tp"), P(("group", "ctx"), "tp")),
        check_vma=False,
    )
```

```python
import functools

import jax
import jax.numpy as jnp
from jax import lax
from jax.experimental import pallas as pl
from jax.experimental.pallas import tpu as pltpu
from jax.sharding import PartitionSpec as P

BLOCK = 64
DH = 128
PIECES = 1
MESH = pl.DeviceIdType.MESH


def dot(a, b, dims):
    return lax.dot_general(a, b, (dims, ((), ())), preferred_element_type=jnp.float32)


NN = ((1,), (0,))
NT = ((1,), (1,))


def kernel(ctx_count, heads, shared, docs, decay, q_hbm, k_hbm, v_hbm, og_hbm, dk, dv,
           q, k, v, g, turned, cum, lead_row, tail_row, factor, factor_other, mine, given, other, sent, later,
           first_out, first_in, handed, back, held, key_inner, value_inner, allowed,
           load_sem, swap_sem, fac_sem, pair_send, pair_recv, first_send, first_recv, chain_send, chain_recv, back_send, back_recv):
    rows = q.shape[0]
    half = og_hbm.shape[0]
    width = q.shape[1]
    owned = (heads - shared) // 2
    steps = owned + shared
    group, ctx, tp = lax.axis_index("group"), lax.axis_index("ctx"), lax.axis_index("tp")
    odd = lax.rem(ctx, 2)
    even = odd == 0
    pair = (group, ctx + 1 - 2 * odd, tp)
    core = (group, ctx, 1 - tp)
    before = (group, ctx - 2, tp)
    after = (group, ctx + 2, tp)
    has_before = ctx >= 2
    has_after = ctx < ctx_count - 2
    windowed = ctx_count <= 8
    if windowed:
        sends_first, gets_first = has_before, has_after
        folds = has_before & (ctx < 4) & has_after
        sends_second = (ctx >= 4) & has_after
        gets_second = has_before & (ctx < ctx_count - 4)
    else:
        sends_second, gets_second = has_before, has_after
    own_base, pair_base = odd * owned, (1 - odd) * owned

    barrier = pltpu.get_barrier_semaphore()
    for peer in (pair, core):
        pl.semaphore_signal(barrier, inc=1, device_id=peer, device_id_type=MESH)

    @pl.when(has_before)
    def _():
        pl.semaphore_signal(barrier, inc=1, device_id=before, device_id_type=MESH)

    @pl.when(has_after)
    def _():
        pl.semaphore_signal(barrier, inc=1, device_id=after, device_id_type=MESH)

    own_rows = pl.ds(pl.multiple_of(tp * half, half), half)
    loads = [pltpu.make_async_copy(src, dst, load_sem.at[i])
             for i, (src, dst) in enumerate((
                 (q_hbm, q),
                 (og_hbm.at[:, pl.ds(pl.multiple_of(tp * width, width), width)], g.at[own_rows, :]),
                 (k_hbm, k), (v_hbm, v)))]
    for copy in loads:
        copy.start()

    blocks = rows // BLOCK
    doc_list = [docs[ctx * blocks + b] for b in range(blocks)]
    first, last = doc_list[0], doc_list[-1]
    prev = docs[jnp.maximum(ctx * blocks - 1, 0)]
    linked = jnp.where((ctx > 0) & (prev == first), 1.0, 0.0).astype(jnp.float32)
    through = jnp.where(first == last, linked, 0.0).astype(jnp.float32)

    def doc_of(position):
        doc = jnp.full(position.shape, first, jnp.int32)
        for b in range(1, blocks):
            doc = jnp.where(position >= b * BLOCK, doc_list[b], doc)
        return doc

    lane = lax.broadcasted_iota(jnp.int32, (heads, rows), 1)
    total = decay[...]
    step = 1
    while step < rows:
        total = total + jnp.where(lane >= step, pltpu.roll(total, step, 1), 0.0)
        step *= 2
    lane_doc = doc_of(lane)
    ending = jnp.broadcast_to(total[:, rows - 1:rows], (heads, rows))
    cum[...] = total
    lead_row[...] = jnp.where(lane_doc == first, jnp.exp(total) * linked, 0.0)
    tail_row[...] = jnp.where(lane_doc == last, jnp.exp(ending - total), 0.0)
    factor[...] = jnp.exp(ending) * through
    key_at = lax.broadcasted_iota(jnp.int32, (rows, rows), 0)
    query_at = lax.broadcasted_iota(jnp.int32, (rows, rows), 1)
    allowed[...] = jnp.where(
        (query_at >= key_at) & (doc_of(query_at) == doc_of(key_at)), 1.0, 0.0)

    def columns(h):
        return pl.ds(pl.multiple_of(h * DH, DH), DH)

    loads[0].wait()

    def turn_step(i, carry):
        for j in range(2):
            h = 2 * i + j
            flipped = q[:, columns(h)].astype(jnp.float32).T
            turned[h] = (flipped * lead_row[pl.ds(h, 1), :]).astype(jnp.bfloat16)
        return carry

    lax.fori_loop(0, heads // 2, turn_step, 0)

    pl.semaphore_wait(barrier, 2 + has_before.astype(jnp.int32) + has_after.astype(jnp.int32))

    swaps = []
    for n, (start, count) in enumerate(((pair_base, owned), (2 * owned, shared), (own_base, owned))):
        if count == 0:
            continue
        theirs = pl.ds(pl.multiple_of((1 - tp) * width + start * DH, DH), count * DH)
        swaps.append(pltpu.make_async_remote_copy(
            src_ref=og_hbm.at[:, theirs],
            dst_ref=g.at[own_rows, pl.ds(pl.multiple_of(start * DH, DH), count * DH)],
            send_sem=swap_sem.at[0, n], recv_sem=swap_sem.at[1, n],
            device_id=core, device_id_type=MESH))
    for swap in swaps:
        swap.start()
    fac_copy = pltpu.make_async_remote_copy(
        src_ref=factor, dst_ref=factor_other, send_sem=fac_sem.at[0], recv_sem=fac_sem.at[1],
        device_id=pair, device_id_type=MESH)
    fac_copy.start()

    piece_rows = DH // PIECES

    def piece(j):
        return pl.ds(j * piece_rows, piece_rows)

    def pair_copy(i, j):
        return pltpu.make_async_remote_copy(
            src_ref=given.at[i, piece(j)], dst_ref=other.at[i, piece(j)],
            send_sem=pair_send.at[i, j], recv_sem=pair_recv.at[i, j],
            device_id=pair, device_id_type=MESH)

    def chain_copy(i, j):
        return pltpu.make_async_remote_copy(
            src_ref=sent.at[i, piece(j)], dst_ref=later.at[i, piece(j)],
            send_sem=chain_send.at[i, j], recv_sem=chain_recv.at[i, j],
            device_id=before, device_id_type=MESH)

    def first_copy(i, j):
        return pltpu.make_async_remote_copy(
            src_ref=first_out.at[i, piece(j)], dst_ref=first_in.at[i, piece(j)],
            send_sem=first_send.at[i, j], recv_sem=first_recv.at[i, j],
            device_id=before, device_id_type=MESH)

    def back_copy(i, j):
        return pltpu.make_async_remote_copy(
            src_ref=handed.at[i, piece(j)], dst_ref=back.at[i, piece(j)],
            send_sem=back_send.at[i, j], recv_sem=back_recv.at[i, j],
            device_id=pair, device_id_type=MESH)

    def state_of(h):
        return dot(turned[h], g[:, columns(h)], NN)

    loads[1].wait()

    def give_step(i, carry):
        given[i] = state_of(pair_base + i).astype(given.dtype)
        for j in range(PIECES):
            pair_copy(i, j).start()
        return carry

    def share_step(i, carry):
        state = state_of(owned + i)
        mine[i] = state
        given[i] = state.astype(given.dtype)
        for j in range(PIECES):
            pair_copy(i, j).start()
        return carry

    def keep_step(i, carry):
        mine[i] = state_of(own_base + i)
        return carry

    swaps[0].wait()
    lax.fori_loop(0, owned, give_step, 0, unroll=2)
    for swap in swaps[1:]:
        swap.wait()
    if shared:
        lax.fori_loop(owned, steps, share_step, 0, unroll=2)
    lax.fori_loop(0, owned, keep_step, 0, unroll=2)
    loads[2].wait()
    loads[3].wait()

    def inner(h):
        cols = columns(h)
        qh, gh = q[:, cols], g[:, cols]
        along = jnp.broadcast_to(cum[pl.ds(h, 1), :], (rows, rows))
        weight = allowed[...] * jnp.exp(jnp.minimum(along - along.T, 0.0))
        mixed_gv = (weight * dot(v[:, cols], gh, NT)).astype(jnp.bfloat16)
        mixed_qk = (weight * dot(k[:, cols], qh, NT)).astype(jnp.bfloat16)
        key_inner[:, cols] = dot(mixed_gv, qh, NN)
        value_inner[:, cols] = dot(mixed_qk, gh, NN)

    def apply(h, state_in):
        cols = columns(h)
        scale = jnp.broadcast_to(tail_row[pl.ds(h, 1), :], (rows, rows)).T
        dk[:, cols] = (key_inner[:, cols] + scale * dot(v[:, cols], state_in, NT)).astype(dk.dtype)
        dv[:, cols] = (value_inner[:, cols] + scale * dot(k[:, cols], state_in, NN)).astype(dv.dtype)

    def early_step(i, carry):
        for j in range(2):
            inner(2 * i + j)
        return carry

    middle = steps if windowed else 0
    early = 4 if windowed else heads - steps
    lax.fori_loop(0, early // 2, early_step, 0)
    fac_copy.wait()

    def parts(i, h, at):
        own_state, pair_state = mine[i, at, :], other[i, at, :].astype(jnp.float32)
        own_factor, pair_factor = factor[pl.ds(h, 1), :], factor_other[pl.ds(h, 1), :]
        state_even = jnp.where(even, own_state, pair_state)
        state_odd = jnp.where(even, pair_state, own_state)
        factor_even = jnp.where(even, own_factor, pair_factor)
        factor_odd = jnp.where(even, pair_factor, own_factor)
        return state_even + factor_even * state_odd, factor_even * factor_odd, state_odd, factor_odd

    def head_of(i):
        return i + jnp.where(i < owned, own_base, owned)

    def first_step(i, carry):
        h = head_of(i)
        for j in range(PIECES):
            at = piece(j)
            pair_copy(i, j).wait_recv()

            @pl.when(folds)
            def _():
                first_copy(i, j).wait_recv()
                joined, both, _, _ = parts(i, h, at)
                first_out[i, at, :] = (joined + both * first_in[i, at, :].astype(jnp.float32)).astype(first_out.dtype)

            @pl.when(sends_first & jnp.logical_not(folds))
            def _():
                first_out[i, at, :] = parts(i, h, at)[0].astype(first_out.dtype)

            @pl.when(sends_first)
            def _():
                first_copy(i, j).start()

        @pl.when(early + i < heads)
        def _():
            inner(early + i)

        return carry

    def chain_piece(i, j):
        h, at = head_of(i), piece(j)
        if windowed:
            @pl.when(gets_first & jnp.logical_not(folds))
            def _():
                first_copy(i, j).wait_recv()
        else:
            pair_copy(i, j).wait_recv()

        @pl.when(gets_second)
        def _():
            chain_copy(i, j).wait_recv()

        incoming = jnp.where(gets_second, later[i, at, :].astype(jnp.float32), 0.0)
        if windowed:
            incoming = jnp.where(
                gets_first & jnp.logical_not(gets_second), first_in[i, at, :].astype(jnp.float32), incoming)
        joined, both, state_odd, factor_odd = parts(i, h, at)

        @pl.when(sends_second)
        def _():
            sent[i, at, :] = (joined + both * incoming).astype(sent.dtype)
            chain_copy(i, j).start()

        into_even = (state_odd + factor_odd * incoming).astype(jnp.bfloat16)
        into_odd = incoming.astype(jnp.bfloat16)

        @pl.when(i < owned)
        def _():
            handed[i, at, :] = jnp.where(even, into_odd, into_even)
            back_copy(i, j).start()

        held[i, at, :] = jnp.where(even, into_even, into_odd)

    def chain_step(i, carry):
        for j in range(PIECES):
            chain_piece(i, j)

        @pl.when(early + middle + i < heads)
        def _():
            inner(early + middle + i)

        return carry

    if windowed:
        lax.fori_loop(0, steps, first_step, 0)
    lax.fori_loop(0, steps, chain_step, 0)

    def own_step(i, carry):
        apply(head_of(i), held[i])
        return carry

    lax.fori_loop(0, steps, own_step, 0, unroll=2)

    def last_step(i, carry):
        for j in range(PIECES):
            back_copy(i, j).wait_recv()
        apply(pair_base + i, back[i])
        return carry

    lax.fori_loop(0, owned, last_step, 0)

    def drain(i, carry):
        for j in range(PIECES):
            pair_copy(i, j).wait_send()

            @pl.when(sends_second)
            def _():
                chain_copy(i, j).wait_send()

            if windowed:
                @pl.when(sends_first)
                def _():
                    first_copy(i, j).wait_send()

            @pl.when(i < owned)
            def _():
                back_copy(i, j).wait_send()

        return carry

    lax.fori_loop(0, steps, drain, 0)


def handover(a_in, b_in, a_out, b_out, sem):
    pieces = sem.shape[1]
    size = a_in.shape[0] // pieces
    moves = [pltpu.make_async_copy(src.at[pl.ds(size * i, size), :], dst.at[pl.ds(size * i, size), :], sem.at[n, i])
             for i in range(pieces) for n, (src, dst) in enumerate(((a_in, a_out), (b_in, b_out)))]
    for move in moves:
        move.start()
    for move in moves:
        move.wait()


def solution(mesh):
    ctx_count = mesh.shape["ctx"]
    wire = jnp.bfloat16 if ctx_count <= 8 else jnp.float32

    def per_device(queries, key_rows, value_rows, out_grad, log_decay, doc_ids):
        rows, features = queries.shape
        heads = log_decay.shape[1]
        shared = 0
        owned = (heads - shared) // 2
        steps = owned + shared
        anywhere = pl.BlockSpec(memory_space=pl.ANY)
        in_vmem = pl.BlockSpec(memory_space=pltpu.VMEM)
        wide = pltpu.VMEM((rows, features), jnp.bfloat16)
        small = pltpu.VMEM((heads, rows), jnp.float32)
        states = pltpu.VMEM((steps, DH, DH), wire)
        total = pltpu.VMEM((rows, features), jnp.float32)
        many = pltpu.SemaphoreType.DMA((steps, PIECES))
        shape = jax.ShapeDtypeStruct((rows, features), jnp.bfloat16)
        inside = pltpu.MemorySpace.VMEM((rows, features), jnp.bfloat16)
        key_grad, value_grad = pl.pallas_call(
            functools.partial(kernel, ctx_count, heads, shared),
            out_shape=(inside, inside),
            in_specs=[pl.BlockSpec(memory_space=pltpu.SMEM), in_vmem] + [anywhere] * 4,
            out_specs=(in_vmem, in_vmem),
            scratch_shapes=[wide] * 4 + [pltpu.VMEM((heads, DH, rows), jnp.bfloat16)] + [small] * 5 + [
                pltpu.VMEM((steps, DH, DH), jnp.float32)] + [states] * 6 + [
                pltpu.VMEM((owned, DH, DH), jnp.bfloat16)] * 2 + [
                pltpu.VMEM((steps, DH, DH), jnp.bfloat16)] + [total] * 2 + [
                pltpu.VMEM((rows, rows), jnp.float32)] + [
                pltpu.SemaphoreType.DMA((4,)), pltpu.SemaphoreType.DMA((2, 3)), pltpu.SemaphoreType.DMA((2,)),
                many, many, many, many, many, many, many, many],
            compiler_params=pltpu.CompilerParams(
                collective_id=0, has_side_effects=True, vmem_limit_bytes=62 << 20),
        )(doc_ids, log_decay.T, queries, key_rows, value_rows, out_grad)
        return tuple(pl.pallas_call(
            handover,
            out_shape=(shape, shape),
            in_specs=[in_vmem] * 2,
            out_specs=(anywhere, anywhere),
            scratch_shapes=[pltpu.SemaphoreType.DMA((2, 4))],
            compiler_params=pltpu.CompilerParams(vmem_limit_bytes=16 << 20),
        )(key_grad, value_grad))

    placed = (
        P(("group", "ctx"), "tp"),
        P(("group", "ctx"), "tp"),
        P(("group", "ctx"), "tp"),
        P(("group", "ctx", "tp"), None),
        P(("group", "ctx"), "tp"),
        P("group"),
    )
    return jax.shard_map(
        per_device,
        mesh=mesh,
        in_specs=placed,
        out_specs=(P(("group", "ctx"), "tp"), P(("group", "ctx"), "tp")),
        check_vma=False,
    )
```

```python
import functools

import jax
import jax.numpy as jnp
from jax import lax
from jax.experimental import pallas as pl
from jax.experimental.pallas import tpu as pltpu
from jax.sharding import PartitionSpec as P

BLOCK = 64
DH = 128
PIECES = 1
MESH = pl.DeviceIdType.MESH


def dot(a, b, dims):
    return lax.dot_general(a, b, (dims, ((), ())), preferred_element_type=jnp.float32)


NN = ((1,), (0,))
NT = ((1,), (1,))


def kernel(ctx_count, heads, shared, docs, decay, q_hbm, k_hbm, v_hbm, og_hbm, dk, dv,
           q, k, v, g, passed, turned, cum, lead_row, tail_row, factor, factor_other, mine, given, other, sent, later,
           first_out, first_in, handed, back, held, key_inner, value_inner, allowed,
           load_sem, swap_sem, fac_sem, pair_send, pair_recv, first_send, first_recv, chain_send, chain_recv, back_send, back_recv):
    rows = q.shape[0]
    half = og_hbm.shape[0]
    width = q.shape[1]
    owned = (heads - shared) // 2
    steps = owned + shared
    group, ctx, tp = lax.axis_index("group"), lax.axis_index("ctx"), lax.axis_index("tp")
    odd = lax.rem(ctx, 2)
    even = odd == 0
    pair = (group, ctx + 1 - 2 * odd, tp)
    core = (group, ctx, 1 - tp)
    before = (group, ctx - 2, tp)
    after = (group, ctx + 2, tp)
    has_before = ctx >= 2
    has_after = ctx < ctx_count - 2
    windowed = ctx_count <= 8
    if windowed:
        sends_first, gets_first = has_before, has_after
        folds = has_before & (ctx < 4) & has_after
        sends_second = (ctx >= 4) & has_after
        gets_second = has_before & (ctx < ctx_count - 4)
    else:
        sends_second, gets_second = has_before, has_after
    own_base, pair_base = odd * owned, (1 - odd) * owned

    barrier = pltpu.get_barrier_semaphore()
    for peer in (pair, core):
        pl.semaphore_signal(barrier, inc=1, device_id=peer, device_id_type=MESH)

    @pl.when(has_after)
    def _():
        pl.semaphore_signal(barrier, inc=1, device_id=after, device_id_type=MESH)

    own_rows = pl.ds(pl.multiple_of(tp * half, half), half)
    loads = [pltpu.make_async_copy(src, dst, load_sem.at[i])
             for i, (src, dst) in enumerate((
                 (q_hbm, q),
                 (og_hbm.at[:, pl.ds(pl.multiple_of(tp * width, width), width)], g.at[own_rows, :]),
                 (og_hbm.at[:, pl.ds(pl.multiple_of((1 - tp) * width, width), width)], passed),
                 (k_hbm, k), (v_hbm, v)))]
    for copy in loads:
        copy.start()

    blocks = rows // BLOCK
    doc_list = [docs[ctx * blocks + b] for b in range(blocks)]
    first, last = doc_list[0], doc_list[-1]
    prev = docs[jnp.maximum(ctx * blocks - 1, 0)]
    linked = jnp.where((ctx > 0) & (prev == first), 1.0, 0.0).astype(jnp.float32)
    through = jnp.where(first == last, linked, 0.0).astype(jnp.float32)

    def doc_of(position):
        doc = jnp.full(position.shape, first, jnp.int32)
        for b in range(1, blocks):
            doc = jnp.where(position >= b * BLOCK, doc_list[b], doc)
        return doc

    lane = lax.broadcasted_iota(jnp.int32, (heads, rows), 1)
    total = decay[...]
    step = 1
    while step < rows:
        total = total + jnp.where(lane >= step, pltpu.roll(total, step, 1), 0.0)
        step *= 2
    lane_doc = doc_of(lane)
    ending = jnp.broadcast_to(total[:, rows - 1:rows], (heads, rows))
    cum[...] = total
    lead_row[...] = jnp.where(lane_doc == first, jnp.exp(total) * linked, 0.0)
    tail_row[...] = jnp.where(lane_doc == last, jnp.exp(ending - total), 0.0)
    factor[...] = jnp.exp(ending) * through
    key_at = lax.broadcasted_iota(jnp.int32, (rows, rows), 0)
    query_at = lax.broadcasted_iota(jnp.int32, (rows, rows), 1)
    allowed[...] = jnp.where(
        (query_at >= key_at) & (doc_of(query_at) == doc_of(key_at)), 1.0, 0.0)

    def columns(h):
        return pl.ds(pl.multiple_of(h * DH, DH), DH)

    loads[0].wait()

    def turn(h):
        flipped = q[:, columns(h)].astype(jnp.float32).T
        return (flipped * lead_row[pl.ds(h, 1), :]).astype(jnp.bfloat16)

    def turn_step(i, carry):
        turned[i] = turn(pair_base + i)
        return carry

    lax.fori_loop(0, owned, turn_step, 0, unroll=2)

    pl.semaphore_wait(barrier, 2 + has_before.astype(jnp.int32))

    loads[2].wait()
    swaps = []
    for n, (start, count) in enumerate(((pair_base, owned), (2 * owned, shared), (own_base, owned))):
        if count == 0:
            continue
        part = pl.ds(pl.multiple_of(start * DH, DH), count * DH)
        swaps.append(pltpu.make_async_remote_copy(
            src_ref=passed.at[:, part], dst_ref=g.at[own_rows, part],
            send_sem=swap_sem.at[0, n], recv_sem=swap_sem.at[1, n],
            device_id=core, device_id_type=MESH))
    for swap in swaps:
        swap.start()
    fac_copy = pltpu.make_async_remote_copy(
        src_ref=factor, dst_ref=factor_other, send_sem=fac_sem.at[0], recv_sem=fac_sem.at[1],
        device_id=pair, device_id_type=MESH)
    fac_copy.start()

    piece_rows = DH // PIECES

    def piece(j):
        return pl.ds(j * piece_rows, piece_rows)

    def pair_copy(i, j):
        return pltpu.make_async_remote_copy(
            src_ref=given.at[i, piece(j)], dst_ref=other.at[i, piece(j)],
            send_sem=pair_send.at[i, j], recv_sem=pair_recv.at[i, j],
            device_id=pair, device_id_type=MESH)

    def chain_copy(i, j):
        return pltpu.make_async_remote_copy(
            src_ref=sent.at[i, piece(j)], dst_ref=later.at[i, piece(j)],
            send_sem=chain_send.at[i, j], recv_sem=chain_recv.at[i, j],
            device_id=before, device_id_type=MESH)

    def first_copy(i, j):
        return pltpu.make_async_remote_copy(
            src_ref=first_out.at[i, piece(j)], dst_ref=first_in.at[i, piece(j)],
            send_sem=first_send.at[i, j], recv_sem=first_recv.at[i, j],
            device_id=before, device_id_type=MESH)

    def back_copy(i, j):
        return pltpu.make_async_remote_copy(
            src_ref=handed.at[i, piece(j)], dst_ref=back.at[i, piece(j)],
            send_sem=back_send.at[i, j], recv_sem=back_recv.at[i, j],
            device_id=pair, device_id_type=MESH)


    loads[1].wait()

    def give_step(i, carry):
        given[i] = dot(turned[i], g[:, columns(pair_base + i)], NN).astype(given.dtype)
        for j in range(PIECES):
            pair_copy(i, j).start()
        return carry

    def share_step(i, carry):
        state = dot(turn(owned + i), g[:, columns(owned + i)], NN)
        mine[i] = state
        given[i] = state.astype(given.dtype)
        for j in range(PIECES):
            pair_copy(i, j).start()
        return carry

    def keep_step(i, carry):
        mine[i] = dot(turn(own_base + i), g[:, columns(own_base + i)], NN)
        return carry

    swaps[0].wait()
    lax.fori_loop(0, owned, give_step, 0, unroll=2)
    for swap in swaps[1:]:
        swap.wait()
    if shared:
        lax.fori_loop(owned, steps, share_step, 0, unroll=2)
    lax.fori_loop(0, owned, keep_step, 0, unroll=2)
    loads[3].wait()
    loads[4].wait()

    def inner(h):
        cols = columns(h)
        qh, gh = q[:, cols], g[:, cols]
        along = jnp.broadcast_to(cum[pl.ds(h, 1), :], (rows, rows))
        weight = allowed[...] * jnp.exp(jnp.minimum(along - along.T, 0.0))
        mixed_gv = (weight * dot(v[:, cols], gh, NT)).astype(jnp.bfloat16)
        mixed_qk = (weight * dot(k[:, cols], qh, NT)).astype(jnp.bfloat16)
        key_inner[:, cols] = dot(mixed_gv, qh, NN)
        value_inner[:, cols] = dot(mixed_qk, gh, NN)

    def apply(h, state_in):
        cols = columns(h)
        scale = jnp.broadcast_to(tail_row[pl.ds(h, 1), :], (rows, rows)).T
        dk[:, cols] = (key_inner[:, cols] + scale * dot(v[:, cols], state_in, NT)).astype(dk.dtype)
        dv[:, cols] = (value_inner[:, cols] + scale * dot(k[:, cols], state_in, NN)).astype(dv.dtype)

    def early_step(i, carry):
        for j in range(2):
            inner(2 * i + j)
        return carry

    middle = steps if windowed else 0
    early = 4 if windowed else heads - steps
    lax.fori_loop(0, early // 2, early_step, 0)
    fac_copy.wait()

    def parts(i, h, at):
        own_state, pair_state = mine[i, at, :], other[i, at, :].astype(jnp.float32)
        own_factor, pair_factor = factor[pl.ds(h, 1), :], factor_other[pl.ds(h, 1), :]
        state_even = jnp.where(even, own_state, pair_state)
        state_odd = jnp.where(even, pair_state, own_state)
        factor_even = jnp.where(even, own_factor, pair_factor)
        factor_odd = jnp.where(even, pair_factor, own_factor)
        return state_even + factor_even * state_odd, factor_even * factor_odd, state_odd, factor_odd

    def head_of(i):
        return i + jnp.where(i < owned, own_base, owned)

    def first_step(i, carry):
        h = head_of(i)
        for j in range(PIECES):
            at = piece(j)
            pair_copy(i, j).wait_recv()

            @pl.when(folds)
            def _():
                first_copy(i, j).wait_recv()
                joined, both, _, _ = parts(i, h, at)
                first_out[i, at, :] = (joined + both * first_in[i, at, :].astype(jnp.float32)).astype(first_out.dtype)

            @pl.when(sends_first & jnp.logical_not(folds))
            def _():
                first_out[i, at, :] = parts(i, h, at)[0].astype(first_out.dtype)

            @pl.when(sends_first)
            def _():
                first_copy(i, j).start()

        @pl.when(early + i < heads)
        def _():
            inner(early + i)

        return carry

    def chain_piece(i, j):
        h, at = head_of(i), piece(j)
        if windowed:
            @pl.when(gets_first & jnp.logical_not(folds))
            def _():
                first_copy(i, j).wait_recv()
        else:
            pair_copy(i, j).wait_recv()

        @pl.when(gets_second)
        def _():
            chain_copy(i, j).wait_recv()

        incoming = jnp.where(gets_second, later[i, at, :].astype(jnp.float32), 0.0)
        if windowed:
            incoming = jnp.where(
                gets_first & jnp.logical_not(gets_second), first_in[i, at, :].astype(jnp.float32), incoming)
        joined, both, state_odd, factor_odd = parts(i, h, at)

        @pl.when(sends_second)
        def _():
            sent[i, at, :] = (joined + both * incoming).astype(sent.dtype)
            chain_copy(i, j).start()

        into_even = (state_odd + factor_odd * incoming).astype(jnp.bfloat16)
        into_odd = incoming.astype(jnp.bfloat16)

        @pl.when(i < owned)
        def _():
            handed[i, at, :] = jnp.where(even, into_odd, into_even)
            back_copy(i, j).start()

        held[i, at, :] = jnp.where(even, into_even, into_odd)

    def chain_step(i, carry):
        for j in range(PIECES):
            chain_piece(i, j)

        @pl.when(early + middle + i < heads)
        def _():
            inner(early + middle + i)

        return carry

    if windowed:
        lax.fori_loop(0, steps, first_step, 0)
    lax.fori_loop(0, steps, chain_step, 0)

    def own_step(i, carry):
        apply(head_of(i), held[i])
        return carry

    lax.fori_loop(0, steps, own_step, 0, unroll=2)

    def last_step(i, carry):
        for j in range(PIECES):
            back_copy(i, j).wait_recv()
        apply(pair_base + i, back[i])
        return carry

    lax.fori_loop(0, owned, last_step, 0)

    def drain(i, carry):
        for j in range(PIECES):
            pair_copy(i, j).wait_send()

            @pl.when(sends_second)
            def _():
                chain_copy(i, j).wait_send()

            if windowed:
                @pl.when(sends_first)
                def _():
                    first_copy(i, j).wait_send()

            @pl.when(i < owned)
            def _():
                back_copy(i, j).wait_send()

        return carry

    lax.fori_loop(0, steps, drain, 0)


def handover(a_in, b_in, a_out, b_out, sem):
    pieces = sem.shape[1]
    size = a_in.shape[0] // pieces
    moves = [pltpu.make_async_copy(src.at[pl.ds(size * i, size), :], dst.at[pl.ds(size * i, size), :], sem.at[n, i])
             for i in range(pieces) for n, (src, dst) in enumerate(((a_in, a_out), (b_in, b_out)))]
    for move in moves:
        move.start()
    for move in moves:
        move.wait()


def solution(mesh):
    ctx_count = mesh.shape["ctx"]
    wire = jnp.bfloat16 if ctx_count <= 8 else jnp.float32

    def per_device(queries, key_rows, value_rows, out_grad, log_decay, doc_ids):
        rows, features = queries.shape
        heads = log_decay.shape[1]
        shared = 0
        owned = (heads - shared) // 2
        steps = owned + shared
        anywhere = pl.BlockSpec(memory_space=pl.ANY)
        in_vmem = pl.BlockSpec(memory_space=pltpu.VMEM)
        wide = pltpu.VMEM((rows, features), jnp.bfloat16)
        small = pltpu.VMEM((heads, rows), jnp.float32)
        states = pltpu.VMEM((steps, DH, DH), wire)
        total = pltpu.VMEM((rows, features), jnp.float32)
        many = pltpu.SemaphoreType.DMA((steps, PIECES))
        shape = jax.ShapeDtypeStruct((rows, features), jnp.bfloat16)
        inside = pltpu.MemorySpace.VMEM((rows, features), jnp.bfloat16)
        key_grad, value_grad = pl.pallas_call(
            functools.partial(kernel, ctx_count, heads, shared),
            out_shape=(inside, inside),
            in_specs=[pl.BlockSpec(memory_space=pltpu.SMEM), in_vmem] + [anywhere] * 4,
            out_specs=(in_vmem, in_vmem),
            scratch_shapes=[wide] * 4 + [pltpu.VMEM((rows // 2, features), jnp.bfloat16), pltpu.VMEM((owned, DH, rows), jnp.bfloat16)] + [small] * 5 + [
                pltpu.VMEM((steps, DH, DH), jnp.float32)] + [states] * 6 + [
                pltpu.VMEM((owned, DH, DH), jnp.bfloat16)] * 2 + [
                pltpu.VMEM((steps, DH, DH), jnp.bfloat16)] + [total] * 2 + [
                pltpu.VMEM((rows, rows), jnp.float32)] + [
                pltpu.SemaphoreType.DMA((5,)), pltpu.SemaphoreType.DMA((2, 3)), pltpu.SemaphoreType.DMA((2,)),
                many, many, many, many, many, many, many, many],
            compiler_params=pltpu.CompilerParams(
                collective_id=0, has_side_effects=True, vmem_limit_bytes=62 << 20),
        )(doc_ids, log_decay.T, queries, key_rows, value_rows, out_grad)
        return tuple(pl.pallas_call(
            handover,
            out_shape=(shape, shape),
            in_specs=[in_vmem] * 2,
            out_specs=(anywhere, anywhere),
            scratch_shapes=[pltpu.SemaphoreType.DMA((2, 4))],
            compiler_params=pltpu.CompilerParams(vmem_limit_bytes=16 << 20),
        )(key_grad, value_grad))

    placed = (
        P(("group", "ctx"), "tp"),
        P(("group", "ctx"), "tp"),
        P(("group", "ctx"), "tp"),
        P(("group", "ctx", "tp"), None),
        P(("group", "ctx"), "tp"),
        P("group"),
    )
    return jax.shard_map(
        per_device,
        mesh=mesh,
        in_specs=placed,
        out_specs=(P(("group", "ctx"), "tp"), P(("group", "ctx"), "tp")),
        check_vma=False,
    )
```

```python
import functools

import jax
import jax.numpy as jnp
from jax import lax
from jax.experimental import pallas as pl
from jax.experimental.pallas import tpu as pltpu
from jax.sharding import PartitionSpec as P

BLOCK = 64
DH = 128
MESH = pl.DeviceIdType.MESH


def dot(a, b, dims):
    return lax.dot_general(a, b, (dims, ((), ())), preferred_element_type=jnp.float32)


NN = ((1,), (0,))
NT = ((1,), (1,))


def kernel(ctx_count, heads, loose, docs, decay, q_hbm, k_hbm, v_hbm, og_hbm, dk, dv,
           q, k, v, g, passed, turned, cum, lead_row, tail_row, factor, factor_other, mine, base, given, other,
           sent, later, first_out, first_in, raw_out, raw_in, late_out, late_in, handed, back, held,
           key_inner, value_inner, allowed,
           load_sem, swap_sem, fac_sem, pair_send, pair_recv, first_send, first_recv, chain_send, chain_recv,
           back_send, back_recv, raw_send, raw_recv, late_send, late_recv):
    rows = q.shape[0]
    half = og_hbm.shape[0]
    width = q.shape[1]
    owned = heads // 2
    kept = owned - loose
    group, ctx, tp = lax.axis_index("group"), lax.axis_index("ctx"), lax.axis_index("tp")
    odd = lax.rem(ctx, 2)
    even = odd == 0
    pair = (group, ctx + 1 - 2 * odd, tp)
    core = (group, ctx, 1 - tp)
    before = (group, ctx - 2, tp)
    after = (group, ctx + 2, tp)
    has_before = ctx >= 2
    has_after = ctx < ctx_count - 2
    windowed = ctx_count <= 8
    if windowed:
        sends_first, gets_first = has_before, has_after
        folds = has_before & (ctx < 4) & has_after
        sends_second = (ctx >= 4) & has_after
        gets_second = has_before & (ctx < ctx_count - 4)
    else:
        sends_second, gets_second = has_before, has_after
    starts_raw = (ctx >= 4) & has_after
    passes_raw = folds if loose else False
    ends_raw = ctx < (2 if loose else 0)
    worked = jnp.where(ends_raw, kept, owned)
    own_base, pair_base = odd * owned, (1 - odd) * owned

    barrier = pltpu.get_barrier_semaphore()
    for peer in (pair, core):
        pl.semaphore_signal(barrier, inc=1, device_id=peer, device_id_type=MESH)

    @pl.when(has_after)
    def _():
        pl.semaphore_signal(barrier, inc=1, device_id=after, device_id_type=MESH)

    own_rows = pl.ds(pl.multiple_of(tp * half, half), half)
    loads = [pltpu.make_async_copy(src, dst, load_sem.at[i])
             for i, (src, dst) in enumerate((
                 (q_hbm, q),
                 (og_hbm.at[:, pl.ds(pl.multiple_of(tp * width, width), width)], g.at[own_rows, :]),
                 (og_hbm.at[:, pl.ds(pl.multiple_of((1 - tp) * width, width), width)], passed),
                 (k_hbm, k), (v_hbm, v)))]
    for copy in loads:
        copy.start()

    blocks = rows // BLOCK
    doc_list = [docs[ctx * blocks + b] for b in range(blocks)]
    first, last = doc_list[0], doc_list[-1]
    prev = docs[jnp.maximum(ctx * blocks - 1, 0)]
    linked = jnp.where((ctx > 0) & (prev == first), 1.0, 0.0).astype(jnp.float32)
    through = jnp.where(first == last, linked, 0.0).astype(jnp.float32)

    def doc_of(position):
        doc = jnp.full(position.shape, first, jnp.int32)
        for b in range(1, blocks):
            doc = jnp.where(position >= b * BLOCK, doc_list[b], doc)
        return doc

    lane = lax.broadcasted_iota(jnp.int32, (heads, rows), 1)
    total = decay[...]
    step = 1
    while step < rows:
        total = total + jnp.where(lane >= step, pltpu.roll(total, step, 1), 0.0)
        step *= 2
    lane_doc = doc_of(lane)
    ending = jnp.broadcast_to(total[:, rows - 1:rows], (heads, rows))
    cum[...] = total
    lead_row[...] = jnp.where(lane_doc == first, jnp.exp(total) * linked, 0.0)
    tail_row[...] = jnp.where(lane_doc == last, jnp.exp(ending - total), 0.0)
    factor[...] = jnp.exp(ending) * through
    key_at = lax.broadcasted_iota(jnp.int32, (rows, rows), 0)
    query_at = lax.broadcasted_iota(jnp.int32, (rows, rows), 1)
    allowed[...] = jnp.where(
        (query_at >= key_at) & (doc_of(query_at) == doc_of(key_at)), 1.0, 0.0)

    def columns(h):
        return pl.ds(pl.multiple_of(h * DH, DH), DH)

    loads[0].wait()

    def turn(h):
        flipped = q[:, columns(h)].astype(jnp.float32).T
        return (flipped * lead_row[pl.ds(h, 1), :]).astype(jnp.bfloat16)

    def turn_step(i, carry):
        turned[i] = turn(pair_base + i)
        return carry

    lax.fori_loop(0, owned, turn_step, 0, unroll=2)

    pl.semaphore_wait(barrier, 2 + has_before.astype(jnp.int32))

    loads[2].wait()
    swaps = []
    for n, start in enumerate((pair_base, own_base)):
        part = pl.ds(pl.multiple_of(start * DH, DH), owned * DH)
        swaps.append(pltpu.make_async_remote_copy(
            src_ref=passed.at[:, part], dst_ref=g.at[own_rows, part],
            send_sem=swap_sem.at[0, n], recv_sem=swap_sem.at[1, n],
            device_id=core, device_id_type=MESH))
    for swap in swaps:
        swap.start()
    fac_copy = pltpu.make_async_remote_copy(
        src_ref=factor, dst_ref=factor_other, send_sem=fac_sem.at[0], recv_sem=fac_sem.at[1],
        device_id=pair, device_id_type=MESH)
    fac_copy.start()

    def remote(src, dst, send, recv, i, peer):
        return pltpu.make_async_remote_copy(
            src_ref=src.at[i], dst_ref=dst.at[i], send_sem=send.at[i], recv_sem=recv.at[i],
            device_id=peer, device_id_type=MESH)

    def pair_copy(i):
        return remote(given, other, pair_send, pair_recv, i, pair)

    def chain_copy(i):
        return remote(sent, later, chain_send, chain_recv, i, before)

    def first_copy(i):
        return remote(first_out, first_in, first_send, first_recv, i, before)

    def raw_copy(i):
        return remote(raw_out, raw_in, raw_send, raw_recv, i, before)

    def late_copy(i):
        return remote(late_out, late_in, late_send, late_recv, i, pair)

    def back_copy(i):
        return remote(handed, back, back_send, back_recv, i, pair)

    def row_of(ref, h):
        return ref[pl.ds(h, 1), :]

    def state_of(h):
        return dot(turn(h), g[:, columns(h)], NN)

    def raw_head(n):
        return n + jnp.where(n < loose, kept, heads - 2 * loose)

    def give_step(i, carry):
        for j in range(2):
            given[2 * i + j] = dot(turned[2 * i + j], g[:, columns(pair_base + 2 * i + j)], NN).astype(given.dtype)
        for j in range(2):
            pair_copy(2 * i + j).start()
        return carry

    def keep_step(i, carry):
        mine[i] = state_of(own_base + i)
        return carry

    loads[1].wait()
    swaps[0].wait()
    ahead = 4 if loose else 0
    lax.fori_loop(0, ahead // 2, give_step, 0)
    if loose:
        swaps[1].wait()

        @pl.when(starts_raw & even)
        def _():
            def step(n, carry):
                raw_out[n] = state_of(raw_head(n)).astype(raw_out.dtype)
                raw_copy(n).start()
                return carry

            lax.fori_loop(0, 2 * loose, step, 0, unroll=2)

        @pl.when(jnp.logical_not(even))
        def _():
            fac_copy.wait_recv()

        @pl.when(starts_raw & jnp.logical_not(even))
        def _():
            def step(n, carry):
                h = raw_head(n)
                raw_out[n] = (state_of(h) * row_of(factor_other, h)).astype(raw_out.dtype)
                raw_copy(n).start()
                return carry

            lax.fori_loop(0, 2 * loose, step, 0, unroll=2)

    lax.fori_loop(ahead // 2, worked // 2, give_step, 0)
    if not loose:
        swaps[1].wait()
    lax.fori_loop(0, owned, keep_step, 0, unroll=2)
    if loose:
        @pl.when(passes_raw | ends_raw)
        def _():
            def step(n, carry):
                base[n] = state_of(raw_head(n))
                return carry

            lax.fori_loop(0, 2 * loose, step, 0, unroll=2)

    loads[3].wait()
    loads[4].wait()

    def inner(h):
        cols = columns(h)
        qh, gh = q[:, cols], g[:, cols]
        along = jnp.broadcast_to(cum[pl.ds(h, 1), :], (rows, rows))
        weight = allowed[...] * jnp.exp(jnp.minimum(along - along.T, 0.0))
        mixed_gv = (weight * dot(v[:, cols], gh, NT)).astype(jnp.bfloat16)
        mixed_qk = (weight * dot(k[:, cols], qh, NT)).astype(jnp.bfloat16)
        key_inner[:, cols] = dot(mixed_gv, qh, NN)
        value_inner[:, cols] = dot(mixed_qk, gh, NN)

    def apply(h, state_in):
        cols = columns(h)
        scale = jnp.broadcast_to(tail_row[pl.ds(h, 1), :], (rows, rows)).T
        dk[:, cols] = (key_inner[:, cols] + scale * dot(v[:, cols], state_in, NT)).astype(dk.dtype)
        dv[:, cols] = (value_inner[:, cols] + scale * dot(k[:, cols], state_in, NN)).astype(dv.dtype)

    def early_step(i, carry):
        for j in range(2):
            inner(2 * i + j)
        return carry

    middle = owned if windowed else 0
    early = 4 if windowed else owned
    lax.fori_loop(0, early // 2, early_step, 0)
    if loose:
        @pl.when(even)
        def _():
            fac_copy.wait_recv()
    else:
        fac_copy.wait_recv()

    def parts(i):
        h = own_base + i
        own_state, pair_state = mine[i], other[i].astype(jnp.float32)
        own_factor, pair_factor = row_of(factor, h), row_of(factor_other, h)
        state_even = jnp.where(even, own_state, pair_state)
        state_odd = jnp.where(even, pair_state, own_state)
        factor_even = jnp.where(even, own_factor, pair_factor)
        factor_odd = jnp.where(even, pair_factor, own_factor)
        return state_even + factor_even * state_odd, factor_even * factor_odd, state_odd, factor_odd

    if loose:
        @pl.when(passes_raw)
        def _():
            def step(n, carry):
                h = raw_head(n)
                pair_factor = row_of(factor_other, h)
                scaled = base[n] * jnp.where(even, 1.0, pair_factor)
                raw_copy(n).wait_recv()
                raw_out[n] = (scaled + (row_of(factor, h) * pair_factor) * raw_in[n].astype(jnp.float32)).astype(
                    raw_out.dtype)
                raw_copy(n).start()
                return carry

            lax.fori_loop(0, 2 * loose, step, 0)

    def between(i):
        @pl.when(i < heads)
        def _():
            inner(i)

    def first_step(i, carry):
        pair_copy(i).wait_recv()

        @pl.when(folds)
        def _():
            first_copy(i).wait_recv()
            joined, both, _, _ = parts(i)
            first_out[i] = (joined + both * first_in[i].astype(jnp.float32)).astype(first_out.dtype)

        @pl.when(sends_first & jnp.logical_not(folds))
        def _():
            first_out[i] = parts(i)[0].astype(first_out.dtype)

        @pl.when(sends_first)
        def _():
            first_copy(i).start()

        between(early + i)
        return carry

    def loose_step(i, carry):
        @pl.when(jnp.logical_not(ends_raw))
        def _():
            pair_copy(i).wait_recv()

        @pl.when(jnp.logical_not(has_after))
        def _():
            first_out[i] = parts(i)[0].astype(first_out.dtype)
            first_copy(i).start()

        between(early + i)
        return carry

    if windowed:
        lax.fori_loop(0, kept, first_step, 0)
        lax.fori_loop(kept, owned, loose_step, 0)

    if loose:
        @pl.when(ends_raw)
        def _():
            def step(n, carry):
                raw_copy(n).wait_recv()
                part = raw_in[n].astype(jnp.float32)
                whole = base[n] + row_of(factor, raw_head(n)) * part
                late_out[n] = jnp.where(even, part, whole).astype(late_out.dtype)
                late_copy(n).start()
                return carry

            lax.fori_loop(0, 2 * loose, step, 0)

    def chain_step(i, carry):
        if windowed:
            @pl.when(gets_first & jnp.logical_not(folds))
            def _():
                first_copy(i).wait_recv()
        else:
            pair_copy(i).wait_recv()

        @pl.when(gets_second)
        def _():
            chain_copy(i).wait_recv()

        incoming = jnp.where(gets_second, later[i].astype(jnp.float32), 0.0)
        if windowed:
            incoming = jnp.where(
                gets_first & jnp.logical_not(gets_second), first_in[i].astype(jnp.float32), incoming)
        joined, both, state_odd, factor_odd = parts(i)

        @pl.when(sends_second)
        def _():
            sent[i] = (joined + both * incoming).astype(sent.dtype)
            chain_copy(i).start()

        into_even = (state_odd + factor_odd * incoming).astype(jnp.bfloat16)
        into_odd = incoming.astype(jnp.bfloat16)
        handed[i] = jnp.where(even, into_odd, into_even)
        back_copy(i).start()
        held[i] = jnp.where(even, into_even, into_odd)
        between(early + middle + i)
        return carry

    lax.fori_loop(0, worked, chain_step, 0)

    if loose:
        @pl.when(ends_raw)
        def _():
            def step(n, carry):
                h = raw_head(n)
                late_copy(n).wait_recv()
                scale = jnp.where(even, row_of(factor_other, h), 1.0)
                apply(h, (late_in[n].astype(jnp.float32) + scale * raw_in[n].astype(jnp.float32)).astype(jnp.bfloat16))
                return carry

            lax.fori_loop(0, 2 * loose, step, 0)

    def own_step(i, carry):
        for j in range(2):
            apply(own_base + 2 * i + j, held[2 * i + j])
        return carry

    lax.fori_loop(0, worked // 2, own_step, 0)

    def last_step(i, carry):
        back_copy(i).wait_recv()
        apply(pair_base + i, back[i])
        return carry

    lax.fori_loop(0, worked, last_step, 0)

    def drain(i, carry):
        pair_copy(i).wait_send()
        back_copy(i).wait_send()

        @pl.when(sends_second)
        def _():
            chain_copy(i).wait_send()

        if windowed:
            @pl.when(sends_first & ((i < kept) | jnp.logical_not(has_after)))
            def _():
                first_copy(i).wait_send()

        return carry

    fac_copy.wait_send()
    lax.fori_loop(0, worked, drain, 0)
    if loose:
        def drain_raw(n, carry):
            @pl.when(starts_raw | passes_raw)
            def _():
                raw_copy(n).wait_send()

            @pl.when(ends_raw)
            def _():
                late_copy(n).wait_send()

            return carry

        lax.fori_loop(0, 2 * loose, drain_raw, 0)


def handover(a_in, b_in, a_out, b_out, sem):
    pieces = sem.shape[1]
    size = a_in.shape[0] // pieces
    moves = [pltpu.make_async_copy(src.at[pl.ds(size * i, size), :], dst.at[pl.ds(size * i, size), :], sem.at[n, i])
             for i in range(pieces) for n, (src, dst) in enumerate(((a_in, a_out), (b_in, b_out)))]
    for move in moves:
        move.start()
    for move in moves:
        move.wait()


def solution(mesh):
    ctx_count = mesh.shape["ctx"]
    wire = jnp.bfloat16 if ctx_count <= 8 else jnp.float32

    def per_device(queries, key_rows, value_rows, out_grad, log_decay, doc_ids):
        rows, features = queries.shape
        heads = log_decay.shape[1]
        owned = heads // 2
        loose = 2 if ctx_count == 8 else 0
        some = max(2 * loose, 1)
        anywhere = pl.BlockSpec(memory_space=pl.ANY)
        in_vmem = pl.BlockSpec(memory_space=pltpu.VMEM)
        wide = pltpu.VMEM((rows, features), jnp.bfloat16)
        small = pltpu.VMEM((heads, rows), jnp.float32)
        states = pltpu.VMEM((owned, DH, DH), wire)
        parts = pltpu.VMEM((some, DH, DH), wire)
        total = pltpu.VMEM((rows, features), jnp.float32)
        many = pltpu.SemaphoreType.DMA((owned,))
        few = pltpu.SemaphoreType.DMA((some,))
        shape = jax.ShapeDtypeStruct((rows, features), jnp.bfloat16)
        inside = pltpu.MemorySpace.VMEM((rows, features), jnp.bfloat16)
        key_grad, value_grad = pl.pallas_call(
            functools.partial(kernel, ctx_count, heads, loose),
            out_shape=(inside, inside),
            in_specs=[pl.BlockSpec(memory_space=pltpu.SMEM), in_vmem] + [anywhere] * 4,
            out_specs=(in_vmem, in_vmem),
            scratch_shapes=[wide] * 4 + [
                pltpu.VMEM((rows // 2, features), jnp.bfloat16),
                pltpu.VMEM((owned, DH, rows), jnp.bfloat16)] + [small] * 5 + [
                pltpu.VMEM((owned, DH, DH), jnp.float32),
                pltpu.VMEM((some, DH, DH), jnp.float32)] + [states] * 6 + [parts] * 4 + [
                pltpu.VMEM((owned, DH, DH), jnp.bfloat16)] * 3 + [total] * 2 + [
                pltpu.VMEM((rows, rows), jnp.float32)] + [
                pltpu.SemaphoreType.DMA((5,)), pltpu.SemaphoreType.DMA((2, 2)), pltpu.SemaphoreType.DMA((2,))] + [
                many] * 8 + [few] * 4,
            compiler_params=pltpu.CompilerParams(
                collective_id=0, has_side_effects=True, vmem_limit_bytes=62 << 20),
        )(doc_ids, log_decay.T, queries, key_rows, value_rows, out_grad)
        return tuple(pl.pallas_call(
            handover,
            out_shape=(shape, shape),
            in_specs=[in_vmem] * 2,
            out_specs=(anywhere, anywhere),
            scratch_shapes=[pltpu.SemaphoreType.DMA((2, 4))],
            compiler_params=pltpu.CompilerParams(vmem_limit_bytes=16 << 20),
        )(key_grad, value_grad))

    placed = (
        P(("group", "ctx"), "tp"),
        P(("group", "ctx"), "tp"),
        P(("group", "ctx"), "tp"),
        P(("group", "ctx", "tp"), None),
        P(("group", "ctx"), "tp"),
        P("group"),
    )
    return jax.shard_map(
        per_device,
        mesh=mesh,
        in_specs=placed,
        out_specs=(P(("group", "ctx"), "tp"), P(("group", "ctx"), "tp")),
        check_vma=False,
    )
```

```python
import functools

import jax
import jax.numpy as jnp
from jax import lax
from jax.experimental import pallas as pl
from jax.experimental.pallas import tpu as pltpu
from jax.sharding import PartitionSpec as P

BLOCK = 64
DH = 128
MESH = pl.DeviceIdType.MESH


def dot(a, b, dims):
    return lax.dot_general(a, b, (dims, ((), ())), preferred_element_type=jnp.float32)


NN = ((1,), (0,))
NT = ((1,), (1,))


def kernel(ctx_count, heads, loose, docs, decay, q_hbm, k_hbm, v_hbm, og_hbm, dk, dv,
           q, k, v, g, passed, turned, cum, lead_row, tail_row, factor, factor_other, mine, given, other,
           sent, later, first_out, first_in, raw_out, raw_in, late_out, late_in, handed, back, held,
           key_inner, value_inner, allowed,
           load_sem, swap_sem, fac_sem, pair_send, pair_recv, first_send, first_recv, chain_send, chain_recv,
           back_send, back_recv, raw_send, raw_recv, late_send, late_recv):
    rows = q.shape[0]
    half = og_hbm.shape[0]
    width = q.shape[1]
    owned = (heads - loose) // 2
    steps = owned + loose
    group, ctx, tp = lax.axis_index("group"), lax.axis_index("ctx"), lax.axis_index("tp")
    odd = lax.rem(ctx, 2)
    even = odd == 0
    pair = (group, ctx + 1 - 2 * odd, tp)
    core = (group, ctx, 1 - tp)
    before = (group, ctx - 2, tp)
    after = (group, ctx + 2, tp)
    has_before = ctx >= 2
    has_after = ctx < ctx_count - 2
    windowed = ctx_count <= 8
    if windowed:
        sends_first, gets_first = has_before, has_after
        folds = has_before & (ctx < 4) & has_after
        sends_second = (ctx >= 4) & has_after
        gets_second = has_before & (ctx < ctx_count - 4)
    else:
        sends_second, gets_second = has_before, has_after
    starts_raw = (ctx >= 4) & has_after
    passes_raw = folds if loose else False
    ends_raw = ctx < (2 if loose else 0)
    own_base, pair_base = odd * owned, (1 - odd) * owned

    barrier = pltpu.get_barrier_semaphore()
    for peer in (pair, core):
        pl.semaphore_signal(barrier, inc=1, device_id=peer, device_id_type=MESH)

    @pl.when(has_after)
    def _():
        pl.semaphore_signal(barrier, inc=1, device_id=after, device_id_type=MESH)

    own_rows = pl.ds(pl.multiple_of(tp * half, half), half)
    loads = [pltpu.make_async_copy(src, dst, load_sem.at[i])
             for i, (src, dst) in enumerate((
                 (q_hbm, q),
                 (og_hbm.at[:, pl.ds(pl.multiple_of(tp * width, width), width)], g.at[own_rows, :]),
                 (og_hbm.at[:, pl.ds(pl.multiple_of((1 - tp) * width, width), width)], passed),
                 (k_hbm, k), (v_hbm, v)))]
    for copy in loads:
        copy.start()

    blocks = rows // BLOCK
    doc_list = [docs[ctx * blocks + b] for b in range(blocks)]
    first, last = doc_list[0], doc_list[-1]
    prev = docs[jnp.maximum(ctx * blocks - 1, 0)]
    linked = jnp.where((ctx > 0) & (prev == first), 1.0, 0.0).astype(jnp.float32)
    through = jnp.where(first == last, linked, 0.0).astype(jnp.float32)

    def doc_of(position):
        doc = jnp.full(position.shape, first, jnp.int32)
        for b in range(1, blocks):
            doc = jnp.where(position >= b * BLOCK, doc_list[b], doc)
        return doc

    lane = lax.broadcasted_iota(jnp.int32, (heads, rows), 1)
    total = decay[...]
    step = 1
    while step < rows:
        total = total + jnp.where(lane >= step, pltpu.roll(total, step, 1), 0.0)
        step *= 2
    lane_doc = doc_of(lane)
    ending = jnp.broadcast_to(total[:, rows - 1:rows], (heads, rows))
    cum[...] = total
    lead_row[...] = jnp.where(lane_doc == first, jnp.exp(total) * linked, 0.0)
    tail_row[...] = jnp.where(lane_doc == last, jnp.exp(ending - total), 0.0)
    factor[...] = jnp.exp(ending) * through
    key_at = lax.broadcasted_iota(jnp.int32, (rows, rows), 0)
    query_at = lax.broadcasted_iota(jnp.int32, (rows, rows), 1)
    allowed[...] = jnp.where(
        (query_at >= key_at) & (doc_of(query_at) == doc_of(key_at)), 1.0, 0.0)

    def columns(h):
        return pl.ds(pl.multiple_of(h * DH, DH), DH)

    loads[0].wait()

    def turn(h):
        flipped = q[:, columns(h)].astype(jnp.float32).T
        return (flipped * lead_row[pl.ds(h, 1), :]).astype(jnp.bfloat16)

    def turn_step(i, carry):
        turned[i] = turn(pair_base + i)
        return carry

    lax.fori_loop(0, owned, turn_step, 0, unroll=2)

    pl.semaphore_wait(barrier, 2 + has_before.astype(jnp.int32))

    loads[2].wait()
    swaps = []
    spread = [(pair_base + m, 2) for m in range(0, owned, 2)] + [(own_base, owned)]
    if loose:
        spread.insert(owned // 2, (2 * owned, loose))
    for n, (start, count) in enumerate(spread):
        part = pl.ds(pl.multiple_of(start * DH, DH), count * DH)
        swaps.append(pltpu.make_async_remote_copy(
            src_ref=passed.at[:, part], dst_ref=g.at[own_rows, part],
            send_sem=swap_sem.at[0, n], recv_sem=swap_sem.at[1, n],
            device_id=core, device_id_type=MESH))
    for swap in swaps:
        swap.start()
    fac_copy = pltpu.make_async_remote_copy(
        src_ref=factor, dst_ref=factor_other, send_sem=fac_sem.at[0], recv_sem=fac_sem.at[1],
        device_id=pair, device_id_type=MESH)
    fac_copy.start()

    def remote(src, dst, send, recv, i, peer):
        return pltpu.make_async_remote_copy(
            src_ref=src.at[i], dst_ref=dst.at[i], send_sem=send.at[i], recv_sem=recv.at[i],
            device_id=peer, device_id_type=MESH)

    def pair_copy(i):
        return remote(given, other, pair_send, pair_recv, i, pair)

    def chain_copy(i):
        return remote(sent, later, chain_send, chain_recv, i, before)

    def first_copy(i):
        return remote(first_out, first_in, first_send, first_recv, i, before)

    def raw_copy(i):
        return remote(raw_out, raw_in, raw_send, raw_recv, i, before)

    def late_copy(i):
        return remote(late_out, late_in, late_send, late_recv, i, pair)

    def back_copy(i):
        return remote(handed, back, back_send, back_recv, i, pair)

    def row_of(ref, h):
        return ref[pl.ds(h, 1), :]

    def state_of(h):
        return dot(turn(h), g[:, columns(h)], NN)

    def give_step(i):
        for j in range(2):
            given[2 * i + j] = dot(turned[2 * i + j], g[:, columns(pair_base + 2 * i + j)], NN).astype(given.dtype)
        for j in range(2):
            pair_copy(2 * i + j).start()

    def keep_step(i, carry):
        mine[i] = state_of(own_base + i)
        return carry

    loads[1].wait()
    ahead = 2
    for i in range(owned // 2):
        if loose and i == ahead:
            swaps[owned // 2].wait()

            @pl.when(jnp.logical_not(even))
            def _():
                fac_copy.wait_recv()

            def loose_step(n, carry):
                h = 2 * owned + n
                state = state_of(h)
                mine[owned + n] = state
                given[owned + n] = state.astype(given.dtype)

                @pl.when(starts_raw & even)
                def _():
                    raw_out[n] = state.astype(raw_out.dtype)

                @pl.when(starts_raw & jnp.logical_not(even))
                def _():
                    raw_out[n] = (state * row_of(factor_other, h)).astype(raw_out.dtype)

                @pl.when(starts_raw)
                def _():
                    raw_copy(n).start()

                return carry

            lax.fori_loop(0, loose, loose_step, 0, unroll=2)
        swaps[i].wait()
        give_step(i)
    if loose:
        @pl.when(jnp.logical_not(ends_raw))
        def _():
            for n in range(loose):
                pair_copy(owned + n).start()

    swaps[-1].wait()
    lax.fori_loop(0, owned, keep_step, 0, unroll=2)
    loads[3].wait()
    loads[4].wait()

    def inner(h):
        cols = columns(h)
        qh, gh = q[:, cols], g[:, cols]
        along = jnp.broadcast_to(cum[pl.ds(h, 1), :], (rows, rows))
        weight = allowed[...] * jnp.exp(jnp.minimum(along - along.T, 0.0))
        mixed_gv = (weight * dot(v[:, cols], gh, NT)).astype(jnp.bfloat16)
        mixed_qk = (weight * dot(k[:, cols], qh, NT)).astype(jnp.bfloat16)
        key_inner[:, cols] = dot(mixed_gv, qh, NN)
        value_inner[:, cols] = dot(mixed_qk, gh, NN)

    def apply(h, state_in):
        cols = columns(h)
        scale = jnp.broadcast_to(tail_row[pl.ds(h, 1), :], (rows, rows)).T
        dk[:, cols] = (key_inner[:, cols] + scale * dot(v[:, cols], state_in, NT)).astype(dk.dtype)
        dv[:, cols] = (value_inner[:, cols] + scale * dot(k[:, cols], state_in, NN)).astype(dv.dtype)

    def early_step(i, carry):
        for j in range(2):
            inner(2 * i + j)
        return carry

    middle = owned if windowed else 0
    early = heads // 2
    if loose:
        early = jnp.where(ends_raw, heads, jnp.where(passes_raw, heads // 2, heads // 4))
    lax.fori_loop(0, early // 2, early_step, 0)
    if loose:
        @pl.when(even)
        def _():
            fac_copy.wait_recv()
    else:
        fac_copy.wait_recv()

    def head_of(i):
        return i + jnp.where(i < owned, own_base, owned)

    def parts(i):
        h = head_of(i)
        own_state, pair_state = mine[i], other[i].astype(jnp.float32)
        own_factor, pair_factor = row_of(factor, h), row_of(factor_other, h)
        state_even = jnp.where(even, own_state, pair_state)
        state_odd = jnp.where(even, pair_state, own_state)
        factor_even = jnp.where(even, own_factor, pair_factor)
        factor_odd = jnp.where(even, pair_factor, own_factor)
        return state_even + factor_even * state_odd, factor_even * factor_odd, state_odd, factor_odd

    if loose:
        @pl.when(passes_raw)
        def _():
            def step(n, carry):
                h = 2 * owned + n
                pair_factor = row_of(factor_other, h)
                scaled = mine[owned + n] * jnp.where(even, 1.0, pair_factor)
                raw_copy(n).wait_recv()
                raw_out[n] = (scaled + (row_of(factor, h) * pair_factor) * raw_in[n].astype(jnp.float32)).astype(
                    raw_out.dtype)
                raw_copy(n).start()
                return carry

            lax.fori_loop(0, loose, step, 0)

    def between(i):
        @pl.when(i < heads)
        def _():
            inner(i)

    def first_step(i, carry):
        pair_copy(i).wait_recv()

        @pl.when(folds)
        def _():
            first_copy(i).wait_recv()
            joined, both, _, _ = parts(i)
            first_out[i] = (joined + both * first_in[i].astype(jnp.float32)).astype(first_out.dtype)

        @pl.when(sends_first & jnp.logical_not(folds))
        def _():
            first_out[i] = parts(i)[0].astype(first_out.dtype)

        @pl.when(sends_first)
        def _():
            first_copy(i).start()

        between(early + i)
        return carry

    if windowed:
        lax.fori_loop(0, owned, first_step, 0)
    if loose:
        @pl.when(jnp.logical_not(has_after))
        def _():
            def step(i, carry):
                pair_copy(i).wait_recv()
                first_out[i] = parts(i)[0].astype(first_out.dtype)
                first_copy(i).start()
                return carry

            lax.fori_loop(owned, steps, step, 0)

    if loose:
        @pl.when(ends_raw)
        def _():
            def step(n, carry):
                raw_copy(n).wait_recv()
                part = raw_in[n].astype(jnp.float32)
                whole = mine[owned + n] + row_of(factor, 2 * owned + n) * part
                late_out[n] = jnp.where(even, part, whole).astype(late_out.dtype)
                late_copy(n).start()
                return carry

            lax.fori_loop(0, loose, step, 0)

    def chain(i):
        if windowed:
            @pl.when(gets_first & jnp.logical_not(folds))
            def _():
                first_copy(i).wait_recv()

        @pl.when(gets_second)
        def _():
            chain_copy(i).wait_recv()

        incoming = jnp.where(gets_second, later[i].astype(jnp.float32), 0.0)
        if windowed:
            incoming = jnp.where(
                gets_first & jnp.logical_not(gets_second), first_in[i].astype(jnp.float32), incoming)
        joined, both, state_odd, factor_odd = parts(i)

        @pl.when(sends_second)
        def _():
            sent[i] = (joined + both * incoming).astype(sent.dtype)
            chain_copy(i).start()

        return (state_odd + factor_odd * incoming).astype(jnp.bfloat16), incoming.astype(jnp.bfloat16)

    def owned_step(i, carry):
        if not windowed:
            pair_copy(i).wait_recv()
        into_even, into_odd = chain(i)
        handed[i] = jnp.where(even, into_odd, into_even)
        back_copy(i).start()
        held[i] = jnp.where(even, into_even, into_odd)
        between(early + middle + i)
        return carry

    if loose:
        @pl.when(sends_second)
        def _():
            for n in range(2):
                pair_copy(owned + n).wait_recv()

    lax.fori_loop(0, owned, owned_step, 0)

    def own_step(i, carry):
        for j in range(2):
            apply(own_base + 2 * i + j, held[2 * i + j])
        return carry

    def apply_own():
        lax.fori_loop(0, owned // 2, own_step, 0)

    if loose:
        @pl.when(ends_raw)
        def _():
            def step(n, carry):
                h = 2 * owned + n
                late_copy(n).wait_recv()
                scale = jnp.where(even, row_of(factor_other, h), 1.0)
                apply(h, (late_in[n].astype(jnp.float32) + scale * raw_in[n].astype(jnp.float32)).astype(jnp.bfloat16))
                return carry

            lax.fori_loop(0, loose, step, 0)

        apply_own()

        @pl.when(jnp.logical_not(ends_raw))
        def _():
            def step(i, carry):
                @pl.when(has_after & jnp.logical_not(sends_second & (i < owned + 2)))
                def _():
                    pair_copy(i).wait_recv()

                into_even, into_odd = chain(i)
                apply(owned + i, jnp.where(even, into_even, into_odd))
                return carry

            lax.fori_loop(owned, steps, step, 0)
    else:
        apply_own()

    def last_step(i, carry):
        back_copy(i).wait_recv()
        apply(pair_base + i, back[i])
        return carry

    lax.fori_loop(0, owned, last_step, 0)

    def drain(i, carry):
        @pl.when((i < owned) | jnp.logical_not(ends_raw))
        def _():
            pair_copy(i).wait_send()

        @pl.when(i < owned)
        def _():
            back_copy(i).wait_send()

        @pl.when(sends_second)
        def _():
            chain_copy(i).wait_send()

        if windowed:
            @pl.when(sends_first & ((i < owned) | jnp.logical_not(has_after)))
            def _():
                first_copy(i).wait_send()

        return carry

    fac_copy.wait_send()
    lax.fori_loop(0, steps, drain, 0)
    if loose:
        def drain_raw(n, carry):
            @pl.when(starts_raw | passes_raw)
            def _():
                raw_copy(n).wait_send()

            @pl.when(ends_raw)
            def _():
                late_copy(n).wait_send()

            return carry

        lax.fori_loop(0, loose, drain_raw, 0)


def handover(a_in, b_in, a_out, b_out, sem):
    pieces = sem.shape[1]
    size = a_in.shape[0] // pieces
    moves = [pltpu.make_async_copy(src.at[pl.ds(size * i, size), :], dst.at[pl.ds(size * i, size), :], sem.at[n, i])
             for i in range(pieces) for n, (src, dst) in enumerate(((a_in, a_out), (b_in, b_out)))]
    for move in moves:
        move.start()
    for move in moves:
        move.wait()


def solution(mesh):
    ctx_count = mesh.shape["ctx"]
    wire = jnp.bfloat16 if ctx_count <= 8 else jnp.float32

    def per_device(queries, key_rows, value_rows, out_grad, log_decay, doc_ids):
        rows, features = queries.shape
        heads = log_decay.shape[1]
        loose = heads // 4 if ctx_count == 8 else 0
        owned = (heads - loose) // 2
        steps = owned + loose
        some = max(loose, 1)
        anywhere = pl.BlockSpec(memory_space=pl.ANY)
        in_vmem = pl.BlockSpec(memory_space=pltpu.VMEM)
        wide = pltpu.VMEM((rows, features), jnp.bfloat16)
        small = pltpu.VMEM((heads, rows), jnp.float32)
        states = pltpu.VMEM((steps, DH, DH), wire)
        parts = pltpu.VMEM((some, DH, DH), wire)
        total = pltpu.VMEM((rows, features), jnp.float32)
        many = pltpu.SemaphoreType.DMA((steps,))
        few = pltpu.SemaphoreType.DMA((some,))
        shape = jax.ShapeDtypeStruct((rows, features), jnp.bfloat16)
        inside = pltpu.MemorySpace.VMEM((rows, features), jnp.bfloat16)
        key_grad, value_grad = pl.pallas_call(
            functools.partial(kernel, ctx_count, heads, loose),
            out_shape=(inside, inside),
            in_specs=[pl.BlockSpec(memory_space=pltpu.SMEM), in_vmem] + [anywhere] * 4,
            out_specs=(in_vmem, in_vmem),
            scratch_shapes=[wide] * 4 + [
                pltpu.VMEM((rows // 2, features), jnp.bfloat16),
                pltpu.VMEM((owned, DH, rows), jnp.bfloat16)] + [small] * 5 + [
                pltpu.VMEM((steps, DH, DH), jnp.float32)] + [states] * 6 + [parts] * 4 + [
                pltpu.VMEM((owned, DH, DH), jnp.bfloat16)] * 3 + [total] * 2 + [
                pltpu.VMEM((rows, rows), jnp.float32)] + [
                pltpu.SemaphoreType.DMA((5,)), pltpu.SemaphoreType.DMA((2, owned // 2 + 2)),
                pltpu.SemaphoreType.DMA((2,))] + [many] * 8 + [few] * 4,
            compiler_params=pltpu.CompilerParams(
                collective_id=0, has_side_effects=True, vmem_limit_bytes=62 << 20),
        )(doc_ids, log_decay.T, queries, key_rows, value_rows, out_grad)
        return tuple(pl.pallas_call(
            handover,
            out_shape=(shape, shape),
            in_specs=[in_vmem] * 2,
            out_specs=(anywhere, anywhere),
            scratch_shapes=[pltpu.SemaphoreType.DMA((2, 4))],
            compiler_params=pltpu.CompilerParams(vmem_limit_bytes=16 << 20),
        )(key_grad, value_grad))

    placed = (
        P(("group", "ctx"), "tp"),
        P(("group", "ctx"), "tp"),
        P(("group", "ctx"), "tp"),
        P(("group", "ctx", "tp"), None),
        P(("group", "ctx"), "tp"),
        P("group"),
    )
    return jax.shard_map(
        per_device,
        mesh=mesh,
        in_specs=placed,
        out_specs=(P(("group", "ctx"), "tp"), P(("group", "ctx"), "tp")),
        check_vma=False,
    )
```

```python
import functools

import jax
import jax.numpy as jnp
from jax import lax
from jax.experimental import pallas as pl
from jax.experimental.pallas import tpu as pltpu
from jax.sharding import PartitionSpec as P

BLOCK = 64
DH = 128
MESH = pl.DeviceIdType.MESH


def dot(a, b, dims):
    return lax.dot_general(a, b, (dims, ((), ())), preferred_element_type=jnp.float32)


NN = ((1,), (0,))
NT = ((1,), (1,))


def kernel(ctx_count, heads, loose, docs, decay, q_hbm, k_hbm, v_hbm, og_hbm, dk, dv,
           q, k, v, g, passed, turned, cum, lead_row, tail_row, factor, factor_other, mine, given, other,
           sent, later, first_out, first_in, raw_out, raw_in, late_out, late_in, handed, back, held,
           key_inner, value_inner, allowed,
           load_sem, swap_sem, fac_sem, pair_send, pair_recv, first_send, first_recv, chain_send, chain_recv,
           back_send, back_recv, raw_send, raw_recv, late_send, late_recv, turn_sem):
    rows = q.shape[0]
    half = og_hbm.shape[0]
    width = q.shape[1]
    owned = (heads - loose) // 2
    steps = owned + loose
    group, ctx, tp = lax.axis_index("group"), lax.axis_index("ctx"), lax.axis_index("tp")
    odd = lax.rem(ctx, 2)
    even = odd == 0
    pair = (group, ctx + 1 - 2 * odd, tp)
    core = (group, ctx, 1 - tp)
    before = (group, ctx - 2, tp)
    after = (group, ctx + 2, tp)
    has_before = ctx >= 2
    has_after = ctx < ctx_count - 2
    windowed = ctx_count <= 8
    if windowed:
        sends_first, gets_first = has_before, has_after
        folds = has_before & (ctx < 4) & has_after
        sends_second = (ctx >= 4) & has_after
        gets_second = has_before & (ctx < ctx_count - 4)
    else:
        sends_second, gets_second = has_before, has_after
    starts_raw = (ctx >= 4) & has_after
    passes_raw = folds if loose else False
    ends_raw = ctx < (2 if loose else 0)
    own_base, pair_base = odd * owned, (1 - odd) * owned

    barrier = pltpu.get_barrier_semaphore()
    for peer in (pair, core):
        pl.semaphore_signal(barrier, inc=1, device_id=peer, device_id_type=MESH)

    @pl.when(has_after)
    def _():
        pl.semaphore_signal(barrier, inc=1, device_id=after, device_id_type=MESH)

    own_rows = pl.ds(pl.multiple_of(tp * half, half), half)
    loads = [pltpu.make_async_copy(src, dst, load_sem.at[i])
             for i, (src, dst) in enumerate((
                 (q_hbm, q),
                 (og_hbm.at[:, pl.ds(pl.multiple_of(tp * width, width), width)], g.at[own_rows, :]),
                 (og_hbm.at[:, pl.ds(pl.multiple_of((1 - tp) * width, width), width)], passed),
                 (k_hbm, k), (v_hbm, v)))]
    for copy in loads:
        copy.start()

    blocks = rows // BLOCK
    doc_list = [docs[ctx * blocks + b] for b in range(blocks)]
    first, last = doc_list[0], doc_list[-1]
    prev = docs[jnp.maximum(ctx * blocks - 1, 0)]
    linked = jnp.where((ctx > 0) & (prev == first), 1.0, 0.0).astype(jnp.float32)
    through = jnp.where(first == last, linked, 0.0).astype(jnp.float32)

    def doc_of(position):
        doc = jnp.full(position.shape, first, jnp.int32)
        for b in range(1, blocks):
            doc = jnp.where(position >= b * BLOCK, doc_list[b], doc)
        return doc

    lane = lax.broadcasted_iota(jnp.int32, (heads, rows), 1)
    total = decay[...]
    step = 1
    while step < rows:
        total = total + jnp.where(lane >= step, pltpu.roll(total, step, 1), 0.0)
        step *= 2
    lane_doc = doc_of(lane)
    ending = jnp.broadcast_to(total[:, rows - 1:rows], (heads, rows))
    cum[...] = total
    lead_row[...] = jnp.where(lane_doc == first, jnp.exp(total) * linked, 0.0)
    tail_row[...] = jnp.where(lane_doc == last, jnp.exp(ending - total), 0.0)
    factor[...] = jnp.exp(ending) * through
    key_at = lax.broadcasted_iota(jnp.int32, (rows, rows), 0)
    query_at = lax.broadcasted_iota(jnp.int32, (rows, rows), 1)
    allowed[...] = jnp.where(
        (query_at >= key_at) & (doc_of(query_at) == doc_of(key_at)), 1.0, 0.0)

    def columns(h):
        return pl.ds(pl.multiple_of(h * DH, DH), DH)

    loads[0].wait()

    def turn(h):
        flipped = q[:, columns(h)].astype(jnp.float32).T
        return (flipped * lead_row[pl.ds(h, 1), :]).astype(jnp.bfloat16)

    def turn_step(i, carry):
        turned[i] = turn(pair_base + i)
        return carry

    lax.fori_loop(0, owned, turn_step, 0, unroll=2)

    pl.semaphore_wait(barrier, 2 + has_before.astype(jnp.int32))

    loads[2].wait()
    swaps = []
    spread = [(pair_base + m, 2) for m in range(0, owned, 2)] + [(own_base, owned)]
    if loose:
        spread.insert(owned // 2, (2 * owned, loose))
    for n, (start, count) in enumerate(spread):
        part = pl.ds(pl.multiple_of(start * DH, DH), count * DH)
        swaps.append(pltpu.make_async_remote_copy(
            src_ref=passed.at[:, part], dst_ref=g.at[own_rows, part],
            send_sem=swap_sem.at[0, n], recv_sem=swap_sem.at[1, n],
            device_id=core, device_id_type=MESH))
    for swap in swaps:
        swap.start()
    fac_copy = pltpu.make_async_remote_copy(
        src_ref=factor, dst_ref=factor_other, send_sem=fac_sem.at[0], recv_sem=fac_sem.at[1],
        device_id=pair, device_id_type=MESH)
    fac_copy.start()

    def remote(src, dst, send, recv, i, peer):
        return pltpu.make_async_remote_copy(
            src_ref=src.at[i], dst_ref=dst.at[i], send_sem=send.at[i], recv_sem=recv.at[i],
            device_id=peer, device_id_type=MESH)

    def pair_copy(i):
        return remote(given, other, pair_send, pair_recv, i, pair)

    def chain_copy(i):
        return remote(sent, later, chain_send, chain_recv, i, before)

    def first_copy(i):
        return remote(first_out, first_in, first_send, first_recv, i, before)

    def raw_copy(i):
        return remote(raw_out, raw_in, raw_send, raw_recv, i, before)

    def late_copy(i):
        return remote(late_out, late_in, late_send, late_recv, i, pair)

    def back_copy(i):
        return remote(handed, back, back_send, back_recv, i, pair)

    def row_of(ref, h):
        return ref[pl.ds(h, 1), :]

    def state_of(h):
        return dot(turn(h), g[:, columns(h)], NN)

    def give_step(i):
        for j in range(2):
            given[2 * i + j] = dot(turned[2 * i + j], g[:, columns(pair_base + 2 * i + j)], NN).astype(given.dtype)
        for j in range(2):
            pair_copy(2 * i + j).start()

    def keep_step(i, carry):
        mine[i] = state_of(own_base + i)
        return carry

    loads[1].wait()
    ahead = 2
    for i in range(owned // 2):
        if loose and i == ahead:
            swaps[owned // 2].wait()

            @pl.when(jnp.logical_not(even))
            def _():
                fac_copy.wait_recv()

            def loose_step(n, carry):
                h = 2 * owned + n
                state = state_of(h)
                mine[owned + n] = state
                given[owned + n] = state.astype(given.dtype)

                @pl.when(starts_raw & even)
                def _():
                    raw_out[n] = state.astype(raw_out.dtype)

                @pl.when(starts_raw & jnp.logical_not(even))
                def _():
                    raw_out[n] = (state * row_of(factor_other, h)).astype(raw_out.dtype)

                @pl.when(starts_raw)
                def _():
                    raw_copy(n).start()

                return carry

            lax.fori_loop(0, loose, loose_step, 0, unroll=2)
        swaps[i].wait()
        give_step(i)
    if loose:
        @pl.when(jnp.logical_not(ends_raw))
        def _():
            for n in range(loose):
                pair_copy(owned + n).start()

    swaps[-1].wait()
    lax.fori_loop(0, owned, keep_step, 0, unroll=2)
    loads[3].wait()
    loads[4].wait()

    def inner(h):
        cols = columns(h)
        qh, gh = q[:, cols], g[:, cols]
        along = jnp.broadcast_to(cum[pl.ds(h, 1), :], (rows, rows))
        weight = allowed[...] * jnp.exp(jnp.minimum(along - along.T, 0.0))
        mixed_gv = (weight * dot(v[:, cols], gh, NT)).astype(jnp.bfloat16)
        mixed_qk = (weight * dot(k[:, cols], qh, NT)).astype(jnp.bfloat16)
        key_inner[:, cols] = dot(mixed_gv, qh, NN)
        value_inner[:, cols] = dot(mixed_qk, gh, NN)

    def apply(h, state_in):
        cols = columns(h)
        scale = jnp.broadcast_to(tail_row[pl.ds(h, 1), :], (rows, rows)).T
        dk[:, cols] = (key_inner[:, cols] + scale * dot(v[:, cols], state_in, NT)).astype(dk.dtype)
        dv[:, cols] = (value_inner[:, cols] + scale * dot(k[:, cols], state_in, NN)).astype(dv.dtype)

    def early_step(i, carry):
        for j in range(2):
            inner(2 * i + j)
        return carry

    middle = owned if windowed else 0
    early = heads // 2
    if loose:
        early = jnp.where(ends_raw, heads, jnp.where(passes_raw, heads // 2, heads // 4))
    lax.fori_loop(0, early // 2, early_step, 0)
    if loose:
        @pl.when(even)
        def _():
            fac_copy.wait_recv()
    else:
        fac_copy.wait_recv()

    def head_of(i):
        return i + jnp.where(i < owned, own_base, owned)

    def parts(i):
        h = head_of(i)
        own_state, pair_state = mine[i], other[i].astype(jnp.float32)
        own_factor, pair_factor = row_of(factor, h), row_of(factor_other, h)
        state_even = jnp.where(even, own_state, pair_state)
        state_odd = jnp.where(even, pair_state, own_state)
        factor_even = jnp.where(even, own_factor, pair_factor)
        factor_odd = jnp.where(even, pair_factor, own_factor)
        return state_even + factor_even * state_odd, factor_even * factor_odd, state_odd, factor_odd

    if loose:
        @pl.when(passes_raw)
        def _():
            def step(n, carry):
                h = 2 * owned + n
                pair_factor = row_of(factor_other, h)
                scaled = mine[owned + n] * jnp.where(even, 1.0, pair_factor)
                raw_copy(n).wait_recv()
                raw_out[n] = (scaled + (row_of(factor, h) * pair_factor) * raw_in[n].astype(jnp.float32)).astype(
                    raw_out.dtype)
                raw_copy(n).start()
                return carry

            lax.fori_loop(0, loose, step, 0)

    def between(i):
        @pl.when(i < heads)
        def _():
            inner(i)

    def first_step(i, carry):
        pair_copy(i).wait_recv()

        @pl.when(folds)
        def _():
            first_copy(i).wait_recv()
            joined, both, _, _ = parts(i)
            first_out[i] = (joined + both * first_in[i].astype(jnp.float32)).astype(first_out.dtype)

        @pl.when(sends_first & jnp.logical_not(folds))
        def _():
            first_out[i] = parts(i)[0].astype(first_out.dtype)

        @pl.when(sends_first)
        def _():
            first_copy(i).start()

        between(early + i)
        return carry

    if windowed:
        lax.fori_loop(0, owned, first_step, 0)
    if loose:
        @pl.when(jnp.logical_not(has_after))
        def _():
            def step(i, carry):
                pair_copy(i).wait_recv()
                first_out[i] = parts(i)[0].astype(first_out.dtype)
                first_copy(i).start()
                return carry

            lax.fori_loop(owned, steps, step, 0)

    if loose:
        @pl.when(ends_raw)
        def _():
            def step(n, carry):
                raw_copy(n).wait_recv()
                part = raw_in[n].astype(jnp.float32)
                whole = mine[owned + n] + row_of(factor, 2 * owned + n) * part
                late_out[n] = jnp.where(even, part, whole).astype(late_out.dtype)
                late_copy(n).start()
                return carry

            lax.fori_loop(0, loose, step, 0)

    def chain(i):
        if windowed:
            @pl.when(gets_first & jnp.logical_not(folds))
            def _():
                first_copy(i).wait_recv()

        @pl.when(gets_second)
        def _():
            chain_copy(i).wait_recv()

        incoming = jnp.where(gets_second, later[i].astype(jnp.float32), 0.0)
        if windowed:
            incoming = jnp.where(
                gets_first & jnp.logical_not(gets_second), first_in[i].astype(jnp.float32), incoming)
        joined, both, state_odd, factor_odd = parts(i)

        @pl.when(sends_second)
        def _():
            sent[i] = (joined + both * incoming).astype(sent.dtype)
            chain_copy(i).start()

        return (state_odd + factor_odd * incoming).astype(jnp.bfloat16), incoming.astype(jnp.bfloat16)

    def raw_result(n):
        h = 2 * owned + n
        late_copy(n).wait_recv()
        scale = jnp.where(even, row_of(factor_other, h), 1.0)
        apply(h, (late_in[n].astype(jnp.float32) + scale * raw_in[n].astype(jnp.float32)).astype(jnp.bfloat16))

    def owned_step(i, carry):
        if not windowed:
            pair_copy(i).wait_recv()
        into_even, into_odd = chain(i)
        handed[i] = jnp.where(even, into_odd, into_even)
        back_copy(i).start()
        held[i] = jnp.where(even, into_even, into_odd)
        if loose:
            @pl.when(ctx < 4)
            def _():
                apply(own_base + i, held[i])

            @pl.when(ends_raw & (i >= owned - loose))
            def _():
                raw_result(i - (owned - loose))

        between(early + middle + i)
        return carry

    if loose:
        @pl.when(sends_second)
        def _():
            for n in range(2):
                pair_copy(owned + n).wait_recv()
            pl.semaphore_signal(turn_sem, inc=1, device_id=core, device_id_type=MESH)
            pl.semaphore_wait(turn_sem, 1)

    lax.fori_loop(0, owned, owned_step, 0)

    def own_step(i, carry):
        for j in range(2):
            apply(own_base + 2 * i + j, held[2 * i + j])
        return carry

    def apply_own():
        lax.fori_loop(0, owned // 2, own_step, 0)

    def drain():
        fac_copy.wait_send()
        for i in range(owned):
            pair_copy(i).wait_send()
        if loose:
            @pl.when(jnp.logical_not(ends_raw))
            def _():
                for i in range(owned, steps):
                    pair_copy(i).wait_send()

            @pl.when(jnp.logical_not(has_after))
            def _():
                for i in range(owned, steps):
                    first_copy(i).wait_send()

            @pl.when(starts_raw | passes_raw)
            def _():
                for n in range(loose):
                    raw_copy(n).wait_send()

            @pl.when(ends_raw)
            def _():
                for n in range(loose):
                    late_copy(n).wait_send()

        if windowed:
            @pl.when(sends_first)
            def _():
                for i in range(owned):
                    first_copy(i).wait_send()

    def last_step(i, carry):
        back_copy(i).wait_recv()
        apply(pair_base + i, back[i])
        return carry

    if loose:
        @pl.when(ctx >= 4)
        def _():
            apply_own()

        drain()
        lax.fori_loop(0, owned - loose, last_step, 0)

        @pl.when(jnp.logical_not(ends_raw))
        def _():
            def step(i, carry):
                @pl.when(has_after & jnp.logical_not(sends_second & (i < owned + 2)))
                def _():
                    pair_copy(i).wait_recv()

                into_even, into_odd = chain(i)
                state_in = jnp.where(even, into_even, into_odd)
                back_copy(i - loose).wait_recv()
                apply(owned + i, state_in)
                apply(pair_base + i - loose, back[i - loose])
                return carry

            lax.fori_loop(owned, steps, step, 0)

        @pl.when(ends_raw)
        def _():
            lax.fori_loop(owned - loose, owned, last_step, 0)
    else:
        apply_own()
        drain()
        lax.fori_loop(0, owned, last_step, 0)

    for i in range(owned):
        back_copy(i).wait_send()

    @pl.when(sends_second)
    def _():
        for i in range(steps):
            chain_copy(i).wait_send()


def handover(a_in, b_in, a_out, b_out, sem):
    pieces = sem.shape[1]
    size = a_in.shape[0] // pieces
    moves = [pltpu.make_async_copy(src.at[pl.ds(size * i, size), :], dst.at[pl.ds(size * i, size), :], sem.at[n, i])
             for i in range(pieces) for n, (src, dst) in enumerate(((a_in, a_out), (b_in, b_out)))]
    for move in moves:
        move.start()
    for move in moves:
        move.wait()


def solution(mesh):
    ctx_count = mesh.shape["ctx"]
    wire = jnp.bfloat16 if ctx_count <= 8 else jnp.float32

    def per_device(queries, key_rows, value_rows, out_grad, log_decay, doc_ids):
        rows, features = queries.shape
        heads = log_decay.shape[1]
        loose = heads // 4 if ctx_count == 8 else 0
        owned = (heads - loose) // 2
        steps = owned + loose
        some = max(loose, 1)
        anywhere = pl.BlockSpec(memory_space=pl.ANY)
        in_vmem = pl.BlockSpec(memory_space=pltpu.VMEM)
        wide = pltpu.VMEM((rows, features), jnp.bfloat16)
        small = pltpu.VMEM((heads, rows), jnp.float32)
        states = pltpu.VMEM((steps, DH, DH), wire)
        parts = pltpu.VMEM((some, DH, DH), wire)
        total = pltpu.VMEM((rows, features), jnp.float32)
        many = pltpu.SemaphoreType.DMA((steps,))
        few = pltpu.SemaphoreType.DMA((some,))
        shape = jax.ShapeDtypeStruct((rows, features), jnp.bfloat16)
        inside = pltpu.MemorySpace.VMEM((rows, features), jnp.bfloat16)
        key_grad, value_grad = pl.pallas_call(
            functools.partial(kernel, ctx_count, heads, loose),
            out_shape=(inside, inside),
            in_specs=[pl.BlockSpec(memory_space=pltpu.SMEM), in_vmem] + [anywhere] * 4,
            out_specs=(in_vmem, in_vmem),
            scratch_shapes=[wide] * 4 + [
                pltpu.VMEM((rows // 2, features), jnp.bfloat16),
                pltpu.VMEM((owned, DH, rows), jnp.bfloat16)] + [small] * 5 + [
                pltpu.VMEM((steps, DH, DH), jnp.float32)] + [states] * 6 + [parts] * 4 + [
                pltpu.VMEM((owned, DH, DH), jnp.bfloat16)] * 3 + [total] * 2 + [
                pltpu.VMEM((rows, rows), jnp.float32)] + [
                pltpu.SemaphoreType.DMA((5,)), pltpu.SemaphoreType.DMA((2, owned // 2 + 2)),
                pltpu.SemaphoreType.DMA((2,))] + [many] * 8 + [few] * 4 + [pltpu.SemaphoreType.REGULAR],
            compiler_params=pltpu.CompilerParams(
                collective_id=0, has_side_effects=True, vmem_limit_bytes=62 << 20),
        )(doc_ids, log_decay.T, queries, key_rows, value_rows, out_grad)
        return tuple(pl.pallas_call(
            handover,
            out_shape=(shape, shape),
            in_specs=[in_vmem] * 2,
            out_specs=(anywhere, anywhere),
            scratch_shapes=[pltpu.SemaphoreType.DMA((2, 4))],
            compiler_params=pltpu.CompilerParams(vmem_limit_bytes=16 << 20),
        )(key_grad, value_grad))

    placed = (
        P(("group", "ctx"), "tp"),
        P(("group", "ctx"), "tp"),
        P(("group", "ctx"), "tp"),
        P(("group", "ctx", "tp"), None),
        P(("group", "ctx"), "tp"),
        P("group"),
    )
    return jax.shard_map(
        per_device,
        mesh=mesh,
        in_specs=placed,
        out_specs=(P(("group", "ctx"), "tp"), P(("group", "ctx"), "tp")),
        check_vma=False,
    )
```

```python
import functools

import jax
import jax.numpy as jnp
from jax import lax
from jax.experimental import pallas as pl
from jax.experimental.pallas import tpu as pltpu
from jax.sharding import PartitionSpec as P

BLOCK = 64
DH = 128
MESH = pl.DeviceIdType.MESH


def dot(a, b, dims):
    return lax.dot_general(a, b, (dims, ((), ())), preferred_element_type=jnp.float32)


NN = ((1,), (0,))
NT = ((1,), (1,))


def kernel(ctx_count, heads, loose, docs, decay, q_hbm, k_hbm, v_hbm, og_hbm, dk, dv,
           q, k, v, g, passed, turned, cum, lead_row, tail_row, factor, factor_other, mine, given, other,
           sent, later, first_out, first_in, raw_out, raw_in, late_out, late_in, handed, back, held,
           key_inner, value_inner, allowed,
           load_sem, swap_sem, fac_sem, pair_send, pair_recv, first_send, first_recv, chain_send, chain_recv,
           back_send, back_recv, raw_send, raw_recv, late_send, late_recv, turn_sem):
    rows = q.shape[0]
    half = og_hbm.shape[0]
    width = q.shape[1]
    owned = (heads - loose) // 2
    steps = owned + loose
    group, ctx, tp = lax.axis_index("group"), lax.axis_index("ctx"), lax.axis_index("tp")
    odd = lax.rem(ctx, 2)
    even = odd == 0
    pair = (group, ctx + 1 - 2 * odd, tp)
    core = (group, ctx, 1 - tp)
    before = (group, ctx - 2, tp)
    after = (group, ctx + 2, tp)
    has_before = ctx >= 2
    has_after = ctx < ctx_count - 2
    windowed = ctx_count <= 8
    if windowed:
        sends_first, gets_first = has_before, has_after
        folds = has_before & (ctx < 4) & has_after
        sends_second = (ctx >= 4) & has_after
        gets_second = has_before & (ctx < ctx_count - 4)
    else:
        sends_second, gets_second = has_before, has_after
    starts_raw = (ctx >= 4) & has_after
    passes_raw = folds if loose else False
    ends_raw = ctx < (2 if loose else 0)
    own_base, pair_base = odd * owned, (1 - odd) * owned

    barrier = pltpu.get_barrier_semaphore()
    for peer in (pair, core):
        pl.semaphore_signal(barrier, inc=1, device_id=peer, device_id_type=MESH)

    @pl.when(has_after)
    def _():
        pl.semaphore_signal(barrier, inc=1, device_id=after, device_id_type=MESH)

    at_start = (ctx == 0) if loose else False
    at_next = (ctx == 1) if loose else False
    at_skip = (ctx == 3) if loose else False
    if loose:
        @pl.when(at_start)
        def _():
            pl.semaphore_signal(barrier, inc=1, device_id=(group, 3, tp), device_id_type=MESH)

    own_rows = pl.ds(pl.multiple_of(tp * half, half), half)
    loads = [pltpu.make_async_copy(src, dst, load_sem.at[i])
             for i, (src, dst) in enumerate((
                 (q_hbm, q),
                 (og_hbm.at[:, pl.ds(pl.multiple_of(tp * width, width), width)], g.at[own_rows, :]),
                 (og_hbm.at[:, pl.ds(pl.multiple_of((1 - tp) * width, width), width)], passed),
                 (k_hbm, k), (v_hbm, v)))]
    for copy in loads:
        copy.start()

    blocks = rows // BLOCK
    doc_list = [docs[ctx * blocks + b] for b in range(blocks)]
    first, last = doc_list[0], doc_list[-1]
    prev = docs[jnp.maximum(ctx * blocks - 1, 0)]
    linked = jnp.where((ctx > 0) & (prev == first), 1.0, 0.0).astype(jnp.float32)
    through = jnp.where(first == last, linked, 0.0).astype(jnp.float32)

    def doc_of(position):
        doc = jnp.full(position.shape, first, jnp.int32)
        for b in range(1, blocks):
            doc = jnp.where(position >= b * BLOCK, doc_list[b], doc)
        return doc

    lane = lax.broadcasted_iota(jnp.int32, (heads, rows), 1)
    total = decay[...]
    step = 1
    while step < rows:
        total = total + jnp.where(lane >= step, pltpu.roll(total, step, 1), 0.0)
        step *= 2
    lane_doc = doc_of(lane)
    ending = jnp.broadcast_to(total[:, rows - 1:rows], (heads, rows))
    cum[...] = total
    lead_row[...] = jnp.where(lane_doc == first, jnp.exp(total) * linked, 0.0)
    tail_row[...] = jnp.where(lane_doc == last, jnp.exp(ending - total), 0.0)
    factor[...] = jnp.exp(ending) * through
    key_at = lax.broadcasted_iota(jnp.int32, (rows, rows), 0)
    query_at = lax.broadcasted_iota(jnp.int32, (rows, rows), 1)
    allowed[...] = jnp.where(
        (query_at >= key_at) & (doc_of(query_at) == doc_of(key_at)), 1.0, 0.0)

    def columns(h):
        return pl.ds(pl.multiple_of(h * DH, DH), DH)

    loads[0].wait()

    def turn(h):
        flipped = q[:, columns(h)].astype(jnp.float32).T
        return (flipped * lead_row[pl.ds(h, 1), :]).astype(jnp.bfloat16)

    def turn_step(i, carry):
        turned[i] = turn(pair_base + i)
        return carry

    lax.fori_loop(0, owned, turn_step, 0, unroll=2)

    arrivals = 2 + has_before.astype(jnp.int32)
    if loose:
        arrivals = arrivals + at_skip.astype(jnp.int32)
    pl.semaphore_wait(barrier, arrivals)

    fac_copy = pltpu.make_async_remote_copy(
        src_ref=factor, dst_ref=factor_other, send_sem=fac_sem.at[0], recv_sem=fac_sem.at[1],
        device_id=pair, device_id_type=MESH)
    fac_copy.start()
    loads[2].wait()
    swaps = []
    spread = [(pair_base + m, 2) for m in range(0, owned, 2)] + [(own_base, owned)]
    if loose:
        spread.insert(owned // 2, (2 * owned, loose))
    for n, (start, count) in enumerate(spread):
        part = pl.ds(pl.multiple_of(start * DH, DH), count * DH)
        swaps.append(pltpu.make_async_remote_copy(
            src_ref=passed.at[:, part], dst_ref=g.at[own_rows, part],
            send_sem=swap_sem.at[0, n], recv_sem=swap_sem.at[1, n],
            device_id=core, device_id_type=MESH))
    for swap in swaps:
        swap.start()

    def remote(src, dst, send, recv, i, peer):
        return pltpu.make_async_remote_copy(
            src_ref=src.at[i], dst_ref=dst.at[i], send_sem=send.at[i], recv_sem=recv.at[i],
            device_id=peer, device_id_type=MESH)

    def pair_copy(i):
        return remote(given, other, pair_send, pair_recv, i, pair)

    def chain_copy(i):
        return remote(sent, later, chain_send, chain_recv, i, before)

    def first_copy(i):
        return remote(first_out, first_in, first_send, first_recv, i, before)

    def raw_copy(i):
        return remote(raw_out, raw_in, raw_send, raw_recv, i, before)

    def late_copy(i):
        return remote(late_out, late_in, late_send, late_recv, i, pair)

    def back_copy(i):
        return remote(handed, back, back_send, back_recv, i, pair)

    skip_copy = pltpu.make_async_remote_copy(
        src_ref=first_out.at[owned - 1], dst_ref=first_in.at[owned], send_sem=first_send.at[owned - 1],
        recv_sem=first_recv.at[owned], device_id=(group, 0, tp), device_id_type=MESH) if loose else None
    extra_copy = pltpu.make_async_remote_copy(
        src_ref=first_in.at[owned], dst_ref=back.at[owned], send_sem=back_send.at[owned],
        recv_sem=back_recv.at[owned], device_id=pair, device_id_type=MESH) if loose else None

    def row_of(ref, h):
        return ref[pl.ds(h, 1), :]

    def state_of(h):
        return dot(turn(h), g[:, columns(h)], NN)

    def give_step(i):
        for j in range(2):
            given[2 * i + j] = dot(turned[2 * i + j], g[:, columns(pair_base + 2 * i + j)], NN).astype(given.dtype)
        for j in range(2):
            pair_copy(2 * i + j).start()

    def keep_step(i, carry):
        mine[i] = state_of(own_base + i)
        return carry

    loads[1].wait()
    ahead = 2
    for i in range(owned // 2):
        if loose and i == ahead:
            swaps[owned // 2].wait()

            @pl.when(jnp.logical_not(even))
            def _():
                fac_copy.wait_recv()

            def loose_step(n, carry):
                h = 2 * owned + n
                state = state_of(h)
                mine[owned + n] = state
                given[owned + n] = state.astype(given.dtype)

                @pl.when(starts_raw & even)
                def _():
                    raw_out[n] = state.astype(raw_out.dtype)

                @pl.when(starts_raw & jnp.logical_not(even))
                def _():
                    raw_out[n] = (state * row_of(factor_other, h)).astype(raw_out.dtype)

                @pl.when(starts_raw)
                def _():
                    raw_copy(n).start()

                return carry

            lax.fori_loop(0, loose, loose_step, 0, unroll=2)
        swaps[i].wait()
        give_step(i)
    if loose:
        @pl.when(jnp.logical_not(ends_raw))
        def _():
            for n in range(loose):
                pair_copy(owned + n).start()

    swaps[-1].wait()
    lax.fori_loop(0, owned, keep_step, 0, unroll=2)
    if loose:
        @pl.when(at_next)
        def _():
            given[owned] = mine[owned - 1].astype(given.dtype)
            pair_copy(owned).start()

    loads[3].wait()
    loads[4].wait()

    def inner(h):
        cols = columns(h)
        qh, gh = q[:, cols], g[:, cols]
        along = jnp.broadcast_to(cum[pl.ds(h, 1), :], (rows, rows))
        weight = allowed[...] * jnp.exp(jnp.minimum(along - along.T, 0.0))
        mixed_gv = (weight * dot(v[:, cols], gh, NT)).astype(jnp.bfloat16)
        mixed_qk = (weight * dot(k[:, cols], qh, NT)).astype(jnp.bfloat16)
        key_inner[:, cols] = dot(mixed_gv, qh, NN)
        value_inner[:, cols] = dot(mixed_qk, gh, NN)

    def apply(h, state_in):
        cols = columns(h)
        scale = jnp.broadcast_to(tail_row[pl.ds(h, 1), :], (rows, rows)).T
        dk[:, cols] = (key_inner[:, cols] + scale * dot(v[:, cols], state_in, NT)).astype(dk.dtype)
        dv[:, cols] = (value_inner[:, cols] + scale * dot(k[:, cols], state_in, NN)).astype(dv.dtype)

    def early_step(i, carry):
        for j in range(2):
            inner(2 * i + j)
        return carry

    middle = owned if windowed else 0
    early = heads // 2
    if loose:
        early = jnp.where(ends_raw, heads, jnp.where(passes_raw, heads // 2, heads // 4))
    lax.fori_loop(0, early // 2, early_step, 0)
    if loose:
        @pl.when(even)
        def _():
            fac_copy.wait_recv()
    else:
        fac_copy.wait_recv()

    def head_of(i):
        return i + jnp.where(i < owned, own_base, owned)

    def parts(i):
        h = head_of(i)
        own_state, pair_state = mine[i], other[i].astype(jnp.float32)
        own_factor, pair_factor = row_of(factor, h), row_of(factor_other, h)
        state_even = jnp.where(even, own_state, pair_state)
        state_odd = jnp.where(even, pair_state, own_state)
        factor_even = jnp.where(even, own_factor, pair_factor)
        factor_odd = jnp.where(even, pair_factor, own_factor)
        return state_even + factor_even * state_odd, factor_even * factor_odd, state_odd, factor_odd

    if loose:
        @pl.when(passes_raw)
        def _():
            def step(n, carry):
                h = 2 * owned + n
                pair_factor = row_of(factor_other, h)
                scaled = mine[owned + n] * jnp.where(even, 1.0, pair_factor)
                raw_copy(n).wait_recv()
                raw_out[n] = (scaled + (row_of(factor, h) * pair_factor) * raw_in[n].astype(jnp.float32)).astype(
                    raw_out.dtype)
                raw_copy(n).start()
                return carry

            lax.fori_loop(0, loose, step, 0)

    def between(i):
        @pl.when(i < heads)
        def _():
            inner(i)

    def first_step(i, carry):
        pair_copy(i).wait_recv()

        @pl.when(folds)
        def _():
            first_copy(i).wait_recv()
            joined, both, _, _ = parts(i)
            first_out[i] = (joined + both * first_in[i].astype(jnp.float32)).astype(first_out.dtype)

        @pl.when(sends_first & jnp.logical_not(folds))
        def _():
            first_out[i] = parts(i)[0].astype(first_out.dtype)

        skips = (at_skip & (i == owned - 1)) if loose else False

        @pl.when(sends_first & jnp.logical_not(skips))
        def _():
            first_copy(i).start()

        if loose:
            @pl.when(skips)
            def _():
                skip_copy.start()

        between(early + i)
        return carry

    if windowed:
        lax.fori_loop(0, owned, first_step, 0)
    if loose:
        @pl.when(jnp.logical_not(has_after))
        def _():
            def step(i, carry):
                pair_copy(i).wait_recv()
                first_out[i] = parts(i)[0].astype(first_out.dtype)
                first_copy(i).start()
                return carry

            lax.fori_loop(owned, steps, step, 0)

    if loose:
        @pl.when(ends_raw)
        def _():
            def step(n, carry):
                raw_copy(n).wait_recv()
                part = raw_in[n].astype(jnp.float32)
                whole = mine[owned + n] + row_of(factor, 2 * owned + n) * part
                late_out[n] = jnp.where(even, part, whole).astype(late_out.dtype)
                late_copy(n).start()
                return carry

            lax.fori_loop(0, loose, step, 0)

    def chain(i):
        if windowed:
            @pl.when(gets_first & jnp.logical_not(folds))
            def _():
                first_copy(i).wait_recv()

        @pl.when(gets_second)
        def _():
            chain_copy(i).wait_recv()

        incoming = jnp.where(gets_second, later[i].astype(jnp.float32), 0.0)
        if windowed:
            incoming = jnp.where(
                gets_first & jnp.logical_not(gets_second), first_in[i].astype(jnp.float32), incoming)
        joined, both, state_odd, factor_odd = parts(i)

        @pl.when(sends_second)
        def _():
            sent[i] = (joined + both * incoming).astype(sent.dtype)
            chain_copy(i).start()

        return (state_odd + factor_odd * incoming).astype(jnp.bfloat16), incoming.astype(jnp.bfloat16)

    def raw_result(n):
        h = 2 * owned + n
        late_copy(n).wait_recv()
        scale = jnp.where(even, row_of(factor_other, h), 1.0)
        apply(h, (late_in[n].astype(jnp.float32) + scale * raw_in[n].astype(jnp.float32)).astype(jnp.bfloat16))

    def owned_step(i, carry):
        if not windowed:
            pair_copy(i).wait_recv()
        into_even, into_odd = chain(i)
        handed[i] = jnp.where(even, into_odd, into_even)
        back_copy(i).start()
        held[i] = jnp.where(even, into_even, into_odd)
        if loose:
            @pl.when(ctx < 4)
            def _():
                apply(own_base + i, held[i])

        between(early + middle + i)
        return carry

    if loose:
        @pl.when(sends_second)
        def _():
            for n in range(1):
                pair_copy(owned + n).wait_recv()
            pl.semaphore_signal(turn_sem, inc=1, device_id=core, device_id_type=MESH)
            pl.semaphore_wait(turn_sem, 1)

    worked = jnp.where(at_next, owned - 1, owned) if loose else owned
    lax.fori_loop(0, worked, owned_step, 0)
    if loose:
        @pl.when(at_start)
        def _():
            skip_copy.wait_recv()
            extra_copy.start()
            pair_copy(owned).wait_recv()
            h = 2 * owned - 1
            whole = other[owned].astype(jnp.float32) + row_of(factor_other, h) * first_in[owned].astype(jnp.float32)
            apply(h, whole.astype(jnp.bfloat16))


    def own_step(i, carry):
        for j in range(2):
            apply(own_base + 2 * i + j, held[2 * i + j])
        return carry

    def apply_own():
        lax.fori_loop(0, owned // 2, own_step, 0)

    def drain():
        fac_copy.wait_send()
        for i in range(owned):
            pair_copy(i).wait_send()
        if loose:
            @pl.when(jnp.logical_not(ends_raw))
            def _():
                for i in range(owned, steps):
                    pair_copy(i).wait_send()

            @pl.when(jnp.logical_not(has_after))
            def _():
                for i in range(owned, steps):
                    first_copy(i).wait_send()

            @pl.when(at_next)
            def _():
                pair_copy(owned).wait_send()

            @pl.when(starts_raw | passes_raw)
            def _():
                for n in range(loose):
                    raw_copy(n).wait_send()

            @pl.when(ends_raw)
            def _():
                for n in range(loose):
                    late_copy(n).wait_send()

        if windowed:
            @pl.when(sends_first)
            def _():
                for i in range(owned):
                    first_copy(i).wait_send()

    def last_step(i, carry):
        back_copy(i).wait_recv()
        apply(pair_base + i, back[i])
        return carry

    if loose:
        @pl.when(ends_raw)
        def _():
            def raw_step(n, carry):
                raw_result(n)
                return carry

            lax.fori_loop(0, loose, raw_step, 0)

        @pl.when(ctx >= 4)
        def _():
            apply_own()

        drain()
        lax.fori_loop(0, owned - loose, last_step, 0)

        @pl.when(jnp.logical_not(ends_raw))
        def _():
            def step(i, carry):
                @pl.when(has_after & jnp.logical_not(sends_second & (i < owned + 1)))
                def _():
                    pair_copy(i).wait_recv()

                into_even, into_odd = chain(i)
                state_in = jnp.where(even, into_even, into_odd)
                back_copy(i - loose).wait_recv()
                apply(owned + i, state_in)
                apply(pair_base + i - loose, back[i - loose])
                return carry

            lax.fori_loop(owned, steps, step, 0)

        @pl.when(ends_raw)
        def _():
            lax.fori_loop(owned - loose, jnp.where(at_start, owned - 1, owned), last_step, 0)

        @pl.when(at_next)
        def _():
            extra_copy.wait_recv()
            apply(2 * owned - 1, back[owned])
    else:
        apply_own()
        drain()
        lax.fori_loop(0, owned, last_step, 0)

    for i in range(owned - 1):
        back_copy(i).wait_send()

    @pl.when(jnp.logical_not(at_next))
    def _():
        back_copy(owned - 1).wait_send()

    if loose:
        @pl.when(at_start)
        def _():
            extra_copy.wait_send()

    @pl.when(sends_second)
    def _():
        for i in range(steps):
            chain_copy(i).wait_send()


def handover(a_in, b_in, a_out, b_out, sem):
    pieces = sem.shape[1]
    size = a_in.shape[0] // pieces
    moves = [pltpu.make_async_copy(src.at[pl.ds(size * i, size), :], dst.at[pl.ds(size * i, size), :], sem.at[n, i])
             for i in range(pieces) for n, (src, dst) in enumerate(((a_in, a_out), (b_in, b_out)))]
    for move in moves:
        move.start()
    for move in moves:
        move.wait()


def solution(mesh):
    ctx_count = mesh.shape["ctx"]
    wire = jnp.bfloat16 if ctx_count <= 8 else jnp.float32

    def per_device(queries, key_rows, value_rows, out_grad, log_decay, doc_ids):
        rows, features = queries.shape
        heads = log_decay.shape[1]
        loose = heads // 4 if ctx_count == 8 else 0
        owned = (heads - loose) // 2
        steps = owned + loose
        some = max(loose, 1)
        anywhere = pl.BlockSpec(memory_space=pl.ANY)
        in_vmem = pl.BlockSpec(memory_space=pltpu.VMEM)
        wide = pltpu.VMEM((rows, features), jnp.bfloat16)
        small = pltpu.VMEM((heads, rows), jnp.float32)
        states = pltpu.VMEM((steps, DH, DH), wire)
        parts = pltpu.VMEM((some, DH, DH), wire)
        total = pltpu.VMEM((rows, features), jnp.float32)
        many = pltpu.SemaphoreType.DMA((steps,))
        few = pltpu.SemaphoreType.DMA((some,))
        shape = jax.ShapeDtypeStruct((rows, features), jnp.bfloat16)
        inside = pltpu.MemorySpace.VMEM((rows, features), jnp.bfloat16)
        key_grad, value_grad = pl.pallas_call(
            functools.partial(kernel, ctx_count, heads, loose),
            out_shape=(inside, inside),
            in_specs=[pl.BlockSpec(memory_space=pltpu.SMEM), in_vmem] + [anywhere] * 4,
            out_specs=(in_vmem, in_vmem),
            scratch_shapes=[wide] * 4 + [
                pltpu.VMEM((rows // 2, features), jnp.bfloat16),
                pltpu.VMEM((owned, DH, rows), jnp.bfloat16)] + [small] * 5 + [
                pltpu.VMEM((steps, DH, DH), jnp.float32)] + [states] * 6 + [parts] * 4 + [
                pltpu.VMEM((owned + 1, DH, DH), jnp.bfloat16)] * 3 + [total] * 2 + [
                pltpu.VMEM((rows, rows), jnp.float32)] + [
                pltpu.SemaphoreType.DMA((5,)), pltpu.SemaphoreType.DMA((2, owned // 2 + 2)),
                pltpu.SemaphoreType.DMA((2,))] + [many] * 8 + [few] * 4 + [pltpu.SemaphoreType.REGULAR],
            compiler_params=pltpu.CompilerParams(
                collective_id=0, has_side_effects=True, vmem_limit_bytes=62 << 20),
        )(doc_ids, log_decay.T, queries, key_rows, value_rows, out_grad)
        return tuple(pl.pallas_call(
            handover,
            out_shape=(shape, shape),
            in_specs=[in_vmem] * 2,
            out_specs=(anywhere, anywhere),
            scratch_shapes=[pltpu.SemaphoreType.DMA((2, 4))],
            compiler_params=pltpu.CompilerParams(vmem_limit_bytes=16 << 20),
        )(key_grad, value_grad))

    placed = (
        P(("group", "ctx"), "tp"),
        P(("group", "ctx"), "tp"),
        P(("group", "ctx"), "tp"),
        P(("group", "ctx", "tp"), None),
        P(("group", "ctx"), "tp"),
        P("group"),
    )
    return jax.shard_map(
        per_device,
        mesh=mesh,
        in_specs=placed,
        out_specs=(P(("group", "ctx"), "tp"), P(("group", "ctx"), "tp")),
        check_vma=False,
    )
```

```python
import functools

import jax
import jax.numpy as jnp
from jax import lax
from jax.experimental import pallas as pl
from jax.experimental.pallas import tpu as pltpu
from jax.sharding import PartitionSpec as P

BLOCK = 64
SKIPPED = 2
DH = 128
MESH = pl.DeviceIdType.MESH


def dot(a, b, dims):
    return lax.dot_general(a, b, (dims, ((), ())), preferred_element_type=jnp.float32)


NN = ((1,), (0,))
NT = ((1,), (1,))


def kernel(ctx_count, heads, loose, docs, decay, q_hbm, k_hbm, v_hbm, og_hbm, dk, dv,
           q, k, v, g, passed, turned, cum, lead_row, tail_row, factor, factor_other, mine, given, other,
           sent, later, first_out, first_in, raw_out, raw_in, late_out, late_in, handed, back, held,
           key_inner, value_inner, allowed,
           load_sem, swap_sem, fac_sem, pair_send, pair_recv, first_send, first_recv, chain_send, chain_recv,
           back_send, back_recv, raw_send, raw_recv, late_send, late_recv, turn_sem):
    rows = q.shape[0]
    half = og_hbm.shape[0]
    width = q.shape[1]
    owned = (heads - loose) // 2
    steps = owned + loose
    group, ctx, tp = lax.axis_index("group"), lax.axis_index("ctx"), lax.axis_index("tp")
    odd = lax.rem(ctx, 2)
    even = odd == 0
    pair = (group, ctx + 1 - 2 * odd, tp)
    core = (group, ctx, 1 - tp)
    before = (group, ctx - 2, tp)
    after = (group, ctx + 2, tp)
    has_before = ctx >= 2
    has_after = ctx < ctx_count - 2
    windowed = ctx_count <= 8
    if windowed:
        sends_first, gets_first = has_before, has_after
        folds = has_before & (ctx < 4) & has_after
        sends_second = (ctx >= 4) & has_after
        gets_second = has_before & (ctx < ctx_count - 4)
    else:
        sends_second, gets_second = has_before, has_after
    starts_raw = (ctx >= 4) & has_after
    passes_raw = folds if loose else False
    ends_raw = ctx < (2 if loose else 0)
    own_base, pair_base = odd * owned, (1 - odd) * owned

    barrier = pltpu.get_barrier_semaphore()
    for peer in (pair, core):
        pl.semaphore_signal(barrier, inc=1, device_id=peer, device_id_type=MESH)

    @pl.when(has_after)
    def _():
        pl.semaphore_signal(barrier, inc=1, device_id=after, device_id_type=MESH)

    at_start = (ctx == 0) if loose else False
    at_next = (ctx == 1) if loose else False
    at_skip = (ctx == 3) if loose else False
    if loose:
        @pl.when(at_start)
        def _():
            pl.semaphore_signal(barrier, inc=1, device_id=(group, 3, tp), device_id_type=MESH)

    own_rows = pl.ds(pl.multiple_of(tp * half, half), half)
    loads = [pltpu.make_async_copy(src, dst, load_sem.at[i])
             for i, (src, dst) in enumerate((
                 (q_hbm, q),
                 (og_hbm.at[:, pl.ds(pl.multiple_of(tp * width, width), width)], g.at[own_rows, :]),
                 (og_hbm.at[:, pl.ds(pl.multiple_of((1 - tp) * width, width), width)], passed),
                 (k_hbm, k), (v_hbm, v)))]
    for copy in loads:
        copy.start()

    blocks = rows // BLOCK
    doc_list = [docs[ctx * blocks + b] for b in range(blocks)]
    first, last = doc_list[0], doc_list[-1]
    prev = docs[jnp.maximum(ctx * blocks - 1, 0)]
    linked = jnp.where((ctx > 0) & (prev == first), 1.0, 0.0).astype(jnp.float32)
    through = jnp.where(first == last, linked, 0.0).astype(jnp.float32)

    def doc_of(position):
        doc = jnp.full(position.shape, first, jnp.int32)
        for b in range(1, blocks):
            doc = jnp.where(position >= b * BLOCK, doc_list[b], doc)
        return doc

    lane = lax.broadcasted_iota(jnp.int32, (heads, rows), 1)
    total = decay[...]
    step = 1
    while step < rows:
        total = total + jnp.where(lane >= step, pltpu.roll(total, step, 1), 0.0)
        step *= 2
    lane_doc = doc_of(lane)
    ending = jnp.broadcast_to(total[:, rows - 1:rows], (heads, rows))
    cum[...] = total
    lead_row[...] = jnp.where(lane_doc == first, jnp.exp(total) * linked, 0.0)
    tail_row[...] = jnp.where(lane_doc == last, jnp.exp(ending - total), 0.0)
    factor[...] = jnp.exp(ending) * through
    key_at = lax.broadcasted_iota(jnp.int32, (rows, rows), 0)
    query_at = lax.broadcasted_iota(jnp.int32, (rows, rows), 1)
    allowed[...] = jnp.where(
        (query_at >= key_at) & (doc_of(query_at) == doc_of(key_at)), 1.0, 0.0)

    def columns(h):
        return pl.ds(pl.multiple_of(h * DH, DH), DH)

    loads[0].wait()

    def turn(h):
        flipped = q[:, columns(h)].astype(jnp.float32).T
        return (flipped * lead_row[pl.ds(h, 1), :]).astype(jnp.bfloat16)

    def turn_step(i, carry):
        turned[i] = turn(pair_base + i)
        return carry

    lax.fori_loop(0, owned, turn_step, 0, unroll=2)

    arrivals = 2 + has_before.astype(jnp.int32)
    if loose:
        arrivals = arrivals + at_skip.astype(jnp.int32)
    pl.semaphore_wait(barrier, arrivals)

    fac_copy = pltpu.make_async_remote_copy(
        src_ref=factor, dst_ref=factor_other, send_sem=fac_sem.at[0], recv_sem=fac_sem.at[1],
        device_id=pair, device_id_type=MESH)
    fac_copy.start()
    loads[2].wait()
    swaps = []
    spread = [(pair_base + m, 2) for m in range(0, owned, 2)] + [(own_base, owned)]
    if loose:
        spread.insert(owned // 2, (2 * owned, loose))
    for n, (start, count) in enumerate(spread):
        part = pl.ds(pl.multiple_of(start * DH, DH), count * DH)
        swaps.append(pltpu.make_async_remote_copy(
            src_ref=passed.at[:, part], dst_ref=g.at[own_rows, part],
            send_sem=swap_sem.at[0, n], recv_sem=swap_sem.at[1, n],
            device_id=core, device_id_type=MESH))
    for swap in swaps:
        swap.start()

    def remote(src, dst, send, recv, i, peer):
        return pltpu.make_async_remote_copy(
            src_ref=src.at[i], dst_ref=dst.at[i], send_sem=send.at[i], recv_sem=recv.at[i],
            device_id=peer, device_id_type=MESH)

    def pair_copy(i):
        return remote(given, other, pair_send, pair_recv, i, pair)

    def chain_copy(i):
        return remote(sent, later, chain_send, chain_recv, i, before)

    def first_copy(i):
        return remote(first_out, first_in, first_send, first_recv, i, before)

    def raw_copy(i):
        return remote(raw_out, raw_in, raw_send, raw_recv, i, before)

    def late_copy(i):
        return remote(late_out, late_in, late_send, late_recv, i, pair)

    def back_copy(i):
        return remote(handed, back, back_send, back_recv, i, pair)

    direct = owned - SKIPPED

    def skip_copy(i):
        return pltpu.make_async_remote_copy(
            src_ref=first_out.at[i], dst_ref=first_in.at[i + SKIPPED], send_sem=first_send.at[i],
            recv_sem=first_recv.at[i + SKIPPED], device_id=(group, 0, tp), device_id_type=MESH)

    def extra_copy(i):
        return remote(first_in, back, back_send, back_recv, i, pair)

    def row_of(ref, h):
        return ref[pl.ds(h, 1), :]

    def state_of(h):
        return dot(turn(h), g[:, columns(h)], NN)

    def give_step(i):
        for j in range(2):
            given[2 * i + j] = dot(turned[2 * i + j], g[:, columns(pair_base + 2 * i + j)], NN).astype(given.dtype)
        for j in range(2):
            pair_copy(2 * i + j).start()

    def keep_step(i, carry):
        mine[i] = state_of(own_base + i)
        return carry

    loads[1].wait()
    ahead = 2
    for i in range(owned // 2):
        if loose and i == ahead:
            swaps[owned // 2].wait()

            @pl.when(jnp.logical_not(even))
            def _():
                fac_copy.wait_recv()

            def loose_step(n, carry):
                h = 2 * owned + n
                state = state_of(h)
                mine[owned + n] = state
                given[owned + n] = state.astype(given.dtype)

                @pl.when(starts_raw & even)
                def _():
                    raw_out[n] = state.astype(raw_out.dtype)

                @pl.when(starts_raw & jnp.logical_not(even))
                def _():
                    raw_out[n] = (state * row_of(factor_other, h)).astype(raw_out.dtype)

                @pl.when(starts_raw)
                def _():
                    raw_copy(n).start()

                return carry

            lax.fori_loop(0, loose, loose_step, 0, unroll=2)
        swaps[i].wait()
        give_step(i)
    if loose:
        @pl.when(jnp.logical_not(ends_raw))
        def _():
            for n in range(loose):
                pair_copy(owned + n).start()

    swaps[-1].wait()
    lax.fori_loop(0, owned, keep_step, 0, unroll=2)
    if loose:
        @pl.when(at_next)
        def _():
            for i in range(owned, owned + SKIPPED):
                given[i] = mine[i - SKIPPED].astype(given.dtype)
                pair_copy(i).start()

    loads[3].wait()
    loads[4].wait()

    def inner(h):
        cols = columns(h)
        qh, gh = q[:, cols], g[:, cols]
        along = jnp.broadcast_to(cum[pl.ds(h, 1), :], (rows, rows))
        weight = allowed[...] * jnp.exp(jnp.minimum(along - along.T, 0.0))
        mixed_gv = (weight * dot(v[:, cols], gh, NT)).astype(jnp.bfloat16)
        mixed_qk = (weight * dot(k[:, cols], qh, NT)).astype(jnp.bfloat16)
        key_inner[:, cols] = dot(mixed_gv, qh, NN)
        value_inner[:, cols] = dot(mixed_qk, gh, NN)

    def apply(h, state_in):
        cols = columns(h)
        scale = jnp.broadcast_to(tail_row[pl.ds(h, 1), :], (rows, rows)).T
        dk[:, cols] = (key_inner[:, cols] + scale * dot(v[:, cols], state_in, NT)).astype(dk.dtype)
        dv[:, cols] = (value_inner[:, cols] + scale * dot(k[:, cols], state_in, NN)).astype(dv.dtype)

    def early_step(i, carry):
        for j in range(2):
            inner(2 * i + j)
        return carry

    middle = owned if windowed else 0
    early = heads // 2
    if loose:
        early = jnp.where(ends_raw, heads, jnp.where(passes_raw, heads // 2, heads // 4))
    lax.fori_loop(0, early // 2, early_step, 0)
    if loose:
        @pl.when(even)
        def _():
            fac_copy.wait_recv()
    else:
        fac_copy.wait_recv()

    def head_of(i):
        return i + jnp.where(i < owned, own_base, owned)

    def parts(i):
        h = head_of(i)
        own_state, pair_state = mine[i], other[i].astype(jnp.float32)
        own_factor, pair_factor = row_of(factor, h), row_of(factor_other, h)
        state_even = jnp.where(even, own_state, pair_state)
        state_odd = jnp.where(even, pair_state, own_state)
        factor_even = jnp.where(even, own_factor, pair_factor)
        factor_odd = jnp.where(even, pair_factor, own_factor)
        return state_even + factor_even * state_odd, factor_even * factor_odd, state_odd, factor_odd

    if loose:
        @pl.when(passes_raw)
        def _():
            def step(n, carry):
                h = 2 * owned + n
                pair_factor = row_of(factor_other, h)
                scaled = mine[owned + n] * jnp.where(even, 1.0, pair_factor)
                raw_copy(n).wait_recv()
                raw_out[n] = (scaled + (row_of(factor, h) * pair_factor) * raw_in[n].astype(jnp.float32)).astype(
                    raw_out.dtype)
                raw_copy(n).start()
                return carry

            lax.fori_loop(0, loose, step, 0)

    def between(i):
        @pl.when(i < heads)
        def _():
            inner(i)

    def first_step(i, carry):
        pair_copy(i).wait_recv()

        @pl.when(folds)
        def _():
            first_copy(i).wait_recv()
            joined, both, _, _ = parts(i)
            first_out[i] = (joined + both * first_in[i].astype(jnp.float32)).astype(first_out.dtype)

        @pl.when(sends_first & jnp.logical_not(folds))
        def _():
            first_out[i] = parts(i)[0].astype(first_out.dtype)

        skips = (at_skip & (i >= direct)) if loose else False

        @pl.when(sends_first & jnp.logical_not(skips))
        def _():
            first_copy(i).start()

        if loose:
            @pl.when(skips)
            def _():
                skip_copy(i).start()

        between(early + i)
        return carry

    if windowed:
        lax.fori_loop(0, owned, first_step, 0)
    if loose:
        @pl.when(jnp.logical_not(has_after))
        def _():
            def step(i, carry):
                pair_copy(i).wait_recv()
                first_out[i] = parts(i)[0].astype(first_out.dtype)
                first_copy(i).start()
                return carry

            lax.fori_loop(owned, steps, step, 0)

    if loose:
        @pl.when(ends_raw)
        def _():
            def step(n, carry):
                raw_copy(n).wait_recv()
                part = raw_in[n].astype(jnp.float32)
                whole = mine[owned + n] + row_of(factor, 2 * owned + n) * part
                late_out[n] = jnp.where(even, part, whole).astype(late_out.dtype)
                late_copy(n).start()
                return carry

            lax.fori_loop(0, loose, step, 0)

    def chain(i):
        if windowed:
            @pl.when(gets_first & jnp.logical_not(folds))
            def _():
                first_copy(i).wait_recv()

        @pl.when(gets_second)
        def _():
            chain_copy(i).wait_recv()

        incoming = jnp.where(gets_second, later[i].astype(jnp.float32), 0.0)
        if windowed:
            incoming = jnp.where(
                gets_first & jnp.logical_not(gets_second), first_in[i].astype(jnp.float32), incoming)
        joined, both, state_odd, factor_odd = parts(i)

        @pl.when(sends_second)
        def _():
            sent[i] = (joined + both * incoming).astype(sent.dtype)
            chain_copy(i).start()

        return (state_odd + factor_odd * incoming).astype(jnp.bfloat16), incoming.astype(jnp.bfloat16)

    def raw_result(n):
        h = 2 * owned + n
        late_copy(n).wait_recv()
        scale = jnp.where(even, row_of(factor_other, h), 1.0)
        apply(h, (late_in[n].astype(jnp.float32) + scale * raw_in[n].astype(jnp.float32)).astype(jnp.bfloat16))

    def owned_step(i, carry):
        if not windowed:
            pair_copy(i).wait_recv()
        into_even, into_odd = chain(i)
        handed[i] = jnp.where(even, into_odd, into_even)
        back_copy(i).start()
        held[i] = jnp.where(even, into_even, into_odd)
        if loose:
            @pl.when(ctx < 4)
            def _():
                apply(own_base + i, held[i])

        between(early + middle + i)
        return carry

    if loose:
        @pl.when(sends_second)
        def _():
            for n in range(1):
                pair_copy(owned + n).wait_recv()
            pl.semaphore_signal(turn_sem, inc=1, device_id=core, device_id_type=MESH)
            pl.semaphore_wait(turn_sem, 1)

    worked = jnp.where(at_next, direct, owned) if loose else owned
    lax.fori_loop(0, worked, owned_step, 0)
    if loose:
        @pl.when(at_start)
        def _():
            for i in range(direct, owned):
                skip_copy(i).wait_recv()
                extra_copy(i + SKIPPED).start()
            for i in range(owned, owned + SKIPPED):
                pair_copy(i).wait_recv()
                h = owned + i - SKIPPED
                whole = other[i].astype(jnp.float32) + row_of(factor_other, h) * first_in[i].astype(jnp.float32)
                apply(h, whole.astype(jnp.bfloat16))


    def own_step(i, carry):
        for j in range(2):
            apply(own_base + 2 * i + j, held[2 * i + j])
        return carry

    def apply_own():
        lax.fori_loop(0, owned // 2, own_step, 0)

    def drain():
        fac_copy.wait_send()
        for i in range(owned):
            pair_copy(i).wait_send()
        if loose:
            @pl.when(jnp.logical_not(ends_raw))
            def _():
                for i in range(owned, steps):
                    pair_copy(i).wait_send()

            @pl.when(jnp.logical_not(has_after))
            def _():
                for i in range(owned, steps):
                    first_copy(i).wait_send()

            @pl.when(at_next)
            def _():
                for i in range(owned, owned + SKIPPED):
                    pair_copy(i).wait_send()

            @pl.when(starts_raw | passes_raw)
            def _():
                for n in range(loose):
                    raw_copy(n).wait_send()

            @pl.when(ends_raw)
            def _():
                for n in range(loose):
                    late_copy(n).wait_send()

        if windowed:
            @pl.when(sends_first)
            def _():
                for i in range(owned):
                    first_copy(i).wait_send()

    def last_step(i, carry):
        back_copy(i).wait_recv()
        apply(pair_base + i, back[i])
        return carry

    if loose:
        @pl.when(ends_raw)
        def _():
            def raw_step(n, carry):
                raw_result(n)
                return carry

            lax.fori_loop(0, loose, raw_step, 0)

        @pl.when(ctx >= 4)
        def _():
            apply_own()

        drain()
        lax.fori_loop(0, owned - loose, last_step, 0)

        @pl.when(jnp.logical_not(ends_raw))
        def _():
            def step(i, carry):
                @pl.when(has_after & jnp.logical_not(sends_second & (i < owned + 1)))
                def _():
                    pair_copy(i).wait_recv()

                into_even, into_odd = chain(i)
                state_in = jnp.where(even, into_even, into_odd)
                back_copy(i - loose).wait_recv()
                apply(owned + i, state_in)
                apply(pair_base + i - loose, back[i - loose])
                return carry

            lax.fori_loop(owned, steps, step, 0)

        @pl.when(ends_raw)
        def _():
            lax.fori_loop(owned - loose, jnp.where(at_start, direct, owned), last_step, 0)

        @pl.when(at_next)
        def _():
            for i in range(owned, owned + SKIPPED):
                extra_copy(i).wait_recv()
                apply(owned + i - SKIPPED, back[i])
    else:
        apply_own()
        drain()
        lax.fori_loop(0, owned, last_step, 0)

    for i in range(direct):
        back_copy(i).wait_send()

    @pl.when(jnp.logical_not(at_next))
    def _():
        for i in range(direct, owned):
            back_copy(i).wait_send()

    if loose:
        @pl.when(at_start)
        def _():
            for i in range(owned, owned + SKIPPED):
                extra_copy(i).wait_send()

    @pl.when(sends_second)
    def _():
        for i in range(steps):
            chain_copy(i).wait_send()


def handover(a_in, b_in, a_out, b_out, sem):
    pieces = sem.shape[1]
    size = a_in.shape[0] // pieces
    moves = [pltpu.make_async_copy(src.at[pl.ds(size * i, size), :], dst.at[pl.ds(size * i, size), :], sem.at[n, i])
             for i in range(pieces) for n, (src, dst) in enumerate(((a_in, a_out), (b_in, b_out)))]
    for move in moves:
        move.start()
    for move in moves:
        move.wait()


def solution(mesh):
    ctx_count = mesh.shape["ctx"]
    wire = jnp.bfloat16 if ctx_count <= 8 else jnp.float32

    def per_device(queries, key_rows, value_rows, out_grad, log_decay, doc_ids):
        rows, features = queries.shape
        heads = log_decay.shape[1]
        loose = heads // 4 if ctx_count == 8 else 0
        owned = (heads - loose) // 2
        steps = owned + loose
        some = max(loose, 1)
        anywhere = pl.BlockSpec(memory_space=pl.ANY)
        in_vmem = pl.BlockSpec(memory_space=pltpu.VMEM)
        wide = pltpu.VMEM((rows, features), jnp.bfloat16)
        small = pltpu.VMEM((heads, rows), jnp.float32)
        states = pltpu.VMEM((steps, DH, DH), wire)
        parts = pltpu.VMEM((some, DH, DH), wire)
        total = pltpu.VMEM((rows, features), jnp.float32)
        many = pltpu.SemaphoreType.DMA((steps,))
        few = pltpu.SemaphoreType.DMA((some,))
        shape = jax.ShapeDtypeStruct((rows, features), jnp.bfloat16)
        inside = pltpu.MemorySpace.VMEM((rows, features), jnp.bfloat16)
        key_grad, value_grad = pl.pallas_call(
            functools.partial(kernel, ctx_count, heads, loose),
            out_shape=(inside, inside),
            in_specs=[pl.BlockSpec(memory_space=pltpu.SMEM), in_vmem] + [anywhere] * 4,
            out_specs=(in_vmem, in_vmem),
            scratch_shapes=[wide] * 4 + [
                pltpu.VMEM((rows // 2, features), jnp.bfloat16),
                pltpu.VMEM((owned, DH, rows), jnp.bfloat16)] + [small] * 5 + [
                pltpu.VMEM((steps, DH, DH), jnp.float32)] + [states] * 6 + [parts] * 4 + [
                pltpu.VMEM((owned + SKIPPED, DH, DH), jnp.bfloat16)] * 3 + [total] * 2 + [
                pltpu.VMEM((rows, rows), jnp.float32)] + [
                pltpu.SemaphoreType.DMA((5,)), pltpu.SemaphoreType.DMA((2, owned // 2 + 2)),
                pltpu.SemaphoreType.DMA((2,))] + [many] * 8 + [few] * 4 + [pltpu.SemaphoreType.REGULAR],
            compiler_params=pltpu.CompilerParams(
                collective_id=0, has_side_effects=True, vmem_limit_bytes=62 << 20),
        )(doc_ids, log_decay.T, queries, key_rows, value_rows, out_grad)
        return tuple(pl.pallas_call(
            handover,
            out_shape=(shape, shape),
            in_specs=[in_vmem] * 2,
            out_specs=(anywhere, anywhere),
            scratch_shapes=[pltpu.SemaphoreType.DMA((2, 4))],
            compiler_params=pltpu.CompilerParams(vmem_limit_bytes=16 << 20),
        )(key_grad, value_grad))

    placed = (
        P(("group", "ctx"), "tp"),
        P(("group", "ctx"), "tp"),
        P(("group", "ctx"), "tp"),
        P(("group", "ctx", "tp"), None),
        P(("group", "ctx"), "tp"),
        P("group"),
    )
    return jax.shard_map(
        per_device,
        mesh=mesh,
        in_specs=placed,
        out_specs=(P(("group", "ctx"), "tp"), P(("group", "ctx"), "tp")),
        check_vma=False,
    )
```

```python
import functools

import jax
import jax.numpy as jnp
from jax import lax
from jax.experimental import pallas as pl
from jax.experimental.pallas import tpu as pltpu
from jax.sharding import PartitionSpec as P

BLOCK = 64
SKIPPED = 2
DH = 128
MESH = pl.DeviceIdType.MESH


def dot(a, b, dims):
    return lax.dot_general(a, b, (dims, ((), ())), preferred_element_type=jnp.float32)


NN = ((1,), (0,))
NT = ((1,), (1,))


def kernel(ctx_count, heads, loose, docs, decay, q_hbm, k_hbm, v_hbm, og_hbm, dk, dv,
           q, k, v, g, passed, turned, cum, lead_row, tail_row, factor, factor_other, mine, given, other,
           sent, later, first_out, first_in, raw_out, raw_in, late_out, late_in, handed, back, held,
           key_inner, value_inner, allowed,
           load_sem, swap_sem, fac_sem, pair_send, pair_recv, first_send, first_recv, chain_send, chain_recv,
           back_send, back_recv, raw_send, raw_recv, late_send, late_recv, turn_sem):
    rows = q.shape[0]
    half = og_hbm.shape[0]
    width = q.shape[1]
    owned = (heads - loose) // 2
    steps = owned + loose
    group, ctx, tp = lax.axis_index("group"), lax.axis_index("ctx"), lax.axis_index("tp")
    odd = lax.rem(ctx, 2)
    even = odd == 0
    pair = (group, ctx + 1 - 2 * odd, tp)
    core = (group, ctx, 1 - tp)
    before = (group, ctx - 2, tp)
    after = (group, ctx + 2, tp)
    has_before = ctx >= 2
    has_after = ctx < ctx_count - 2
    windowed = ctx_count <= 8
    if windowed:
        sends_first, gets_first = has_before, has_after
        folds = has_before & (ctx < 4) & has_after
        sends_second = (ctx >= 4) & has_after
        gets_second = has_before & (ctx < ctx_count - 4)
    else:
        sends_second, gets_second = has_before, has_after
    starts_raw = (ctx >= 4) & has_after
    passes_raw = folds if loose else False
    ends_raw = ctx < (2 if loose else 0)
    own_base, pair_base = odd * owned, (1 - odd) * owned

    barrier = pltpu.get_barrier_semaphore()
    for peer in (pair, core):
        pl.semaphore_signal(barrier, inc=1, device_id=peer, device_id_type=MESH)

    @pl.when(has_after)
    def _():
        pl.semaphore_signal(barrier, inc=1, device_id=after, device_id_type=MESH)

    at_start = (ctx == 0) if loose else False
    at_next = (ctx == 1) if loose else False
    at_skip = (ctx == 3) if loose else False
    if loose:
        @pl.when(at_start)
        def _():
            pl.semaphore_signal(barrier, inc=1, device_id=(group, 3, tp), device_id_type=MESH)

    own_rows = pl.ds(pl.multiple_of(tp * half, half), half)
    loads = [pltpu.make_async_copy(src, dst, load_sem.at[i])
             for i, (src, dst) in enumerate((
                 (q_hbm, q),
                 (og_hbm.at[:, pl.ds(pl.multiple_of(tp * width, width), width)], g.at[own_rows, :]),
                 (og_hbm.at[:, pl.ds(pl.multiple_of((1 - tp) * width, width), width)], passed),
                 (k_hbm, k), (v_hbm, v)))]
    for copy in loads:
        copy.start()

    blocks = rows // BLOCK
    doc_list = [docs[ctx * blocks + b] for b in range(blocks)]
    first, last = doc_list[0], doc_list[-1]
    prev = docs[jnp.maximum(ctx * blocks - 1, 0)]
    linked = jnp.where((ctx > 0) & (prev == first), 1.0, 0.0).astype(jnp.float32)
    through = jnp.where(first == last, linked, 0.0).astype(jnp.float32)

    def doc_of(position):
        doc = jnp.full(position.shape, first, jnp.int32)
        for b in range(1, blocks):
            doc = jnp.where(position >= b * BLOCK, doc_list[b], doc)
        return doc

    lane = lax.broadcasted_iota(jnp.int32, (heads, rows), 1)
    total = decay[...]
    step = 1
    while step < rows:
        total = total + jnp.where(lane >= step, pltpu.roll(total, step, 1), 0.0)
        step *= 2
    lane_doc = doc_of(lane)
    ending = jnp.broadcast_to(total[:, rows - 1:rows], (heads, rows))
    cum[...] = total
    lead_row[...] = jnp.where(lane_doc == first, jnp.exp(total) * linked, 0.0)
    tail_row[...] = jnp.where(lane_doc == last, jnp.exp(ending - total), 0.0)
    factor[...] = jnp.exp(ending) * through
    key_at = lax.broadcasted_iota(jnp.int32, (rows, rows), 0)
    query_at = lax.broadcasted_iota(jnp.int32, (rows, rows), 1)
    allowed[...] = jnp.where(
        (query_at >= key_at) & (doc_of(query_at) == doc_of(key_at)), 1.0, 0.0)

    def columns(h):
        return pl.ds(pl.multiple_of(h * DH, DH), DH)

    loads[0].wait()

    def turn(h):
        flipped = q[:, columns(h)].astype(jnp.float32).T
        return (flipped * lead_row[pl.ds(h, 1), :]).astype(jnp.bfloat16)

    def turn_step(i, carry):
        turned[i] = turn(pair_base + i)
        return carry

    lax.fori_loop(0, owned, turn_step, 0, unroll=2)

    arrivals = 2 + has_before.astype(jnp.int32)
    if loose:
        arrivals = arrivals + at_skip.astype(jnp.int32)
    pl.semaphore_wait(barrier, arrivals)

    fac_copy = pltpu.make_async_remote_copy(
        src_ref=factor, dst_ref=factor_other, send_sem=fac_sem.at[0], recv_sem=fac_sem.at[1],
        device_id=pair, device_id_type=MESH)
    fac_copy.start()
    loads[2].wait()
    swaps = []
    spread = [(pair_base + m, 2) for m in range(0, owned, 2)] + [(own_base, owned)]
    if loose:
        spread.insert(owned // 2, (2 * owned, loose))
    for n, (start, count) in enumerate(spread):
        part = pl.ds(pl.multiple_of(start * DH, DH), count * DH)
        swaps.append(pltpu.make_async_remote_copy(
            src_ref=passed.at[:, part], dst_ref=g.at[own_rows, part],
            send_sem=swap_sem.at[0, n], recv_sem=swap_sem.at[1, n],
            device_id=core, device_id_type=MESH))
    for swap in swaps:
        swap.start()

    def remote(src, dst, send, recv, i, peer):
        return pltpu.make_async_remote_copy(
            src_ref=src.at[i], dst_ref=dst.at[i], send_sem=send.at[i], recv_sem=recv.at[i],
            device_id=peer, device_id_type=MESH)

    def pair_copy(i):
        return remote(given, other, pair_send, pair_recv, i, pair)

    def chain_copy(i):
        return remote(sent, later, chain_send, chain_recv, i, before)

    def first_copy(i):
        return remote(first_out, first_in, first_send, first_recv, i, before)

    def raw_copy(i):
        return remote(raw_out, raw_in, raw_send, raw_recv, i, before)

    def late_copy(i):
        return remote(late_out, late_in, late_send, late_recv, i, pair)

    def back_copy(i):
        return remote(handed, back, back_send, back_recv, i, pair)

    direct = owned - SKIPPED

    def skip_copy(i):
        return pltpu.make_async_remote_copy(
            src_ref=first_out.at[i], dst_ref=first_in.at[i + SKIPPED], send_sem=first_send.at[i],
            recv_sem=first_recv.at[i + SKIPPED], device_id=(group, 0, tp), device_id_type=MESH)

    def extra_copy(i):
        return remote(first_in, back, back_send, back_recv, i, pair)

    def row_of(ref, h):
        return ref[pl.ds(h, 1), :]

    def state_of(h):
        return dot(turn(h), g[:, columns(h)], NN)

    def give_step(i):
        for j in range(2):
            given[2 * i + j] = dot(turned[2 * i + j], g[:, columns(pair_base + 2 * i + j)], NN).astype(given.dtype)
        for j in range(2):
            pair_copy(2 * i + j).start()

    def keep_step(i, carry):
        mine[i] = state_of(own_base + i)
        return carry

    loads[1].wait()
    ahead = 2
    for i in range(owned // 2):
        if loose and i == ahead:
            swaps[owned // 2].wait()

            @pl.when(jnp.logical_not(even))
            def _():
                fac_copy.wait_recv()

            def loose_step(n, carry):
                h = 2 * owned + n
                state = state_of(h)
                mine[owned + n] = state
                given[owned + n] = state.astype(given.dtype)

                @pl.when(starts_raw & even)
                def _():
                    raw_out[n] = state.astype(raw_out.dtype)

                @pl.when(starts_raw & jnp.logical_not(even))
                def _():
                    raw_out[n] = (state * row_of(factor_other, h)).astype(raw_out.dtype)

                @pl.when(starts_raw)
                def _():
                    raw_copy(n).start()

                return carry

            lax.fori_loop(0, loose, loose_step, 0, unroll=2)
        swaps[i].wait()
        give_step(i)
    if loose:
        @pl.when(jnp.logical_not(ends_raw))
        def _():
            for n in range(loose):
                pair_copy(owned + n).start()

    swaps[-1].wait()
    lax.fori_loop(0, owned, keep_step, 0, unroll=2)
    if loose:
        @pl.when(at_next)
        def _():
            for i in range(owned, owned + SKIPPED):
                given[i] = mine[i - SKIPPED].astype(given.dtype)
                pair_copy(i).start()

    loads[3].wait()
    loads[4].wait()

    def inner(h):
        cols = columns(h)
        qh, gh = q[:, cols], g[:, cols]
        along = jnp.broadcast_to(cum[pl.ds(h, 1), :], (rows, rows))
        weight = allowed[...] * jnp.exp(jnp.minimum(along - along.T, 0.0))
        mixed_gv = (weight * dot(v[:, cols], gh, NT)).astype(jnp.bfloat16)
        mixed_qk = (weight * dot(k[:, cols], qh, NT)).astype(jnp.bfloat16)
        key_inner[:, cols] = dot(mixed_gv, qh, NN)
        value_inner[:, cols] = dot(mixed_qk, gh, NN)

    def apply(h, state_in):
        cols = columns(h)
        scale = jnp.broadcast_to(tail_row[pl.ds(h, 1), :], (rows, rows)).T
        dk[:, cols] = (key_inner[:, cols] + scale * dot(v[:, cols], state_in, NT)).astype(dk.dtype)
        dv[:, cols] = (value_inner[:, cols] + scale * dot(k[:, cols], state_in, NN)).astype(dv.dtype)

    def early_step(i, carry):
        for j in range(2):
            inner(2 * i + j)
        return carry

    middle = owned if windowed else 0
    early = heads // 2
    if loose:
        early = jnp.where(ends_raw, heads, jnp.where(passes_raw, heads // 2, heads // 4))
    lax.fori_loop(0, early // 2, early_step, 0)
    if loose:
        @pl.when(even)
        def _():
            fac_copy.wait_recv()
    else:
        fac_copy.wait_recv()

    def head_of(i):
        return i + jnp.where(i < owned, own_base, owned)

    def parts(i):
        h = head_of(i)
        own_state, pair_state = mine[i], other[i].astype(jnp.float32)
        own_factor, pair_factor = row_of(factor, h), row_of(factor_other, h)
        state_even = jnp.where(even, own_state, pair_state)
        state_odd = jnp.where(even, pair_state, own_state)
        factor_even = jnp.where(even, own_factor, pair_factor)
        factor_odd = jnp.where(even, pair_factor, own_factor)
        return state_even + factor_even * state_odd, factor_even * factor_odd, state_odd, factor_odd

    if loose:
        @pl.when(passes_raw)
        def _():
            def step(n, carry):
                h = 2 * owned + n
                pair_factor = row_of(factor_other, h)
                scaled = mine[owned + n] * jnp.where(even, 1.0, pair_factor)
                raw_copy(n).wait_recv()
                raw_out[n] = (scaled + (row_of(factor, h) * pair_factor) * raw_in[n].astype(jnp.float32)).astype(
                    raw_out.dtype)
                raw_copy(n).start()
                return carry

            lax.fori_loop(0, loose, step, 0)

    def between(i):
        @pl.when(i < heads)
        def _():
            inner(i)

    def first_step(i, carry):
        pair_copy(i).wait_recv()

        @pl.when(folds)
        def _():
            first_copy(i).wait_recv()
            joined, both, _, _ = parts(i)
            first_out[i] = (joined + both * first_in[i].astype(jnp.float32)).astype(first_out.dtype)

        @pl.when(sends_first & jnp.logical_not(folds))
        def _():
            first_out[i] = parts(i)[0].astype(first_out.dtype)

        skips = (at_skip & (i >= direct)) if loose else False

        @pl.when(sends_first & jnp.logical_not(skips))
        def _():
            first_copy(i).start()

        if loose:
            @pl.when(skips)
            def _():
                skip_copy(i).start()

        between(early + i)
        return carry

    if windowed:
        lax.fori_loop(0, owned, first_step, 0)
    if loose:
        @pl.when(jnp.logical_not(has_after))
        def _():
            def step(i, carry):
                pair_copy(i).wait_recv()
                first_out[i] = parts(i)[0].astype(first_out.dtype)
                first_copy(i).start()
                return carry

            lax.fori_loop(owned, steps, step, 0)

    if loose:
        @pl.when(ends_raw)
        def _():
            def step(n, carry):
                raw_copy(n).wait_recv()
                part = raw_in[n].astype(jnp.float32)
                whole = mine[owned + n] + row_of(factor, 2 * owned + n) * part
                late_out[n] = jnp.where(even, part, whole).astype(late_out.dtype)
                late_copy(n).start()
                return carry

            lax.fori_loop(0, loose, step, 0)

    def chain(i):
        if windowed:
            @pl.when(gets_first & jnp.logical_not(folds))
            def _():
                first_copy(i).wait_recv()

        @pl.when(gets_second)
        def _():
            chain_copy(i).wait_recv()

        incoming = jnp.where(gets_second, later[i].astype(jnp.float32), 0.0)
        if windowed:
            incoming = jnp.where(
                gets_first & jnp.logical_not(gets_second), first_in[i].astype(jnp.float32), incoming)
        joined, both, state_odd, factor_odd = parts(i)

        @pl.when(sends_second)
        def _():
            sent[i] = (joined + both * incoming).astype(sent.dtype)
            chain_copy(i).start()

        return (state_odd + factor_odd * incoming).astype(jnp.bfloat16), incoming.astype(jnp.bfloat16)

    def raw_result(n):
        h = 2 * owned + n
        late_copy(n).wait_recv()
        scale = jnp.where(even, row_of(factor_other, h), 1.0)
        apply(h, (late_in[n].astype(jnp.float32) + scale * raw_in[n].astype(jnp.float32)).astype(jnp.bfloat16))

    def owned_step(i, carry):
        if not windowed:
            pair_copy(i).wait_recv()
        into_even, into_odd = chain(i)
        handed[i] = jnp.where(even, into_odd, into_even)
        back_copy(i).start()
        held[i] = jnp.where(even, into_even, into_odd)
        if loose:
            @pl.when(ctx < 4)
            def _():
                apply(own_base + i, held[i])

        between(early + middle + i)
        return carry

    if loose:
        @pl.when(sends_second)
        def _():
            for n in range(1):
                pair_copy(owned + n).wait_recv()
            pl.semaphore_signal(turn_sem, inc=1, device_id=core, device_id_type=MESH)
            pl.semaphore_wait(turn_sem, 1)

    worked = jnp.where(at_next, direct, owned) if loose else owned
    lax.fori_loop(0, worked, owned_step, 0)
    if loose:
        @pl.when(at_start)
        def _():
            for i in range(direct, owned):
                skip_copy(i).wait_recv()
                extra_copy(i + SKIPPED).start()
            for i in range(owned, owned + SKIPPED):
                pair_copy(i).wait_recv()
                h = owned + i - SKIPPED
                whole = other[i].astype(jnp.float32) + row_of(factor_other, h) * first_in[i].astype(jnp.float32)
                apply(h, whole.astype(jnp.bfloat16))


    def own_step(i, carry):
        for j in range(2):
            apply(own_base + 2 * i + j, held[2 * i + j])
        return carry

    def apply_own():
        lax.fori_loop(0, owned // 2, own_step, 0)

    def drain():
        fac_copy.wait_send()
        for i in range(owned):
            pair_copy(i).wait_send()
        if loose:
            @pl.when(jnp.logical_not(ends_raw))
            def _():
                for i in range(owned, steps):
                    pair_copy(i).wait_send()

            @pl.when(jnp.logical_not(has_after))
            def _():
                for i in range(owned, steps):
                    first_copy(i).wait_send()

            @pl.when(at_next)
            def _():
                for i in range(owned, owned + SKIPPED):
                    pair_copy(i).wait_send()

            @pl.when(starts_raw | passes_raw)
            def _():
                for n in range(loose):
                    raw_copy(n).wait_send()

            @pl.when(ends_raw)
            def _():
                for n in range(loose):
                    late_copy(n).wait_send()

        if windowed:
            @pl.when(sends_first)
            def _():
                for i in range(owned):
                    first_copy(i).wait_send()

    def last_step(i, carry):
        back_copy(i).wait_recv()
        apply(pair_base + i, back[i])
        return carry

    if loose:
        @pl.when(ends_raw)
        def _():
            def raw_step(n, carry):
                raw_result(n)
                return carry

            lax.fori_loop(0, loose, raw_step, 0)

        @pl.when(ctx >= 4)
        def _():
            apply_own()

        drain()
        lax.fori_loop(0, owned - loose, last_step, 0)

        @pl.when(jnp.logical_not(ends_raw))
        def _():
            def step(i, carry):
                @pl.when(has_after & jnp.logical_not(sends_second & (i < owned + 1)))
                def _():
                    pair_copy(i).wait_recv()

                into_even, into_odd = chain(i)
                state_in = jnp.where(even, into_even, into_odd)
                back_copy(i - loose).wait_recv()
                apply(owned + i, state_in)
                apply(pair_base + i - loose, back[i - loose])
                return carry

            lax.fori_loop(owned, steps, step, 0)

        @pl.when(ends_raw)
        def _():
            lax.fori_loop(owned - loose, jnp.where(at_start, direct, owned), last_step, 0)

        @pl.when(at_next)
        def _():
            for i in range(owned, owned + SKIPPED):
                extra_copy(i).wait_recv()
                apply(owned + i - SKIPPED, back[i])
    else:
        apply_own()
        drain()
        lax.fori_loop(0, owned, last_step, 0)

    for i in range(direct):
        back_copy(i).wait_send()

    @pl.when(jnp.logical_not(at_next))
    def _():
        for i in range(direct, owned):
            back_copy(i).wait_send()

    if loose:
        @pl.when(at_start)
        def _():
            for i in range(owned, owned + SKIPPED):
                extra_copy(i).wait_send()

    @pl.when(sends_second)
    def _():
        for i in range(steps):
            chain_copy(i).wait_send()


def handover(a_in, b_in, a_out, b_out, sem):
    pieces = sem.shape[1]
    size = a_in.shape[0] // pieces
    moves = [pltpu.make_async_copy(src.at[pl.ds(size * i, size), :], dst.at[pl.ds(size * i, size), :], sem.at[n, i])
             for i in range(pieces) for n, (src, dst) in enumerate(((a_in, a_out), (b_in, b_out)))]
    for n, move in enumerate(moves):
        move.start(priority=n % 2)
    for move in moves:
        move.wait()


def solution(mesh):
    ctx_count = mesh.shape["ctx"]
    wire = jnp.bfloat16 if ctx_count <= 8 else jnp.float32

    def per_device(queries, key_rows, value_rows, out_grad, log_decay, doc_ids):
        rows, features = queries.shape
        heads = log_decay.shape[1]
        loose = heads // 4 if ctx_count == 8 else 0
        owned = (heads - loose) // 2
        steps = owned + loose
        some = max(loose, 1)
        anywhere = pl.BlockSpec(memory_space=pl.ANY)
        in_vmem = pl.BlockSpec(memory_space=pltpu.VMEM)
        wide = pltpu.VMEM((rows, features), jnp.bfloat16)
        small = pltpu.VMEM((heads, rows), jnp.float32)
        states = pltpu.VMEM((steps, DH, DH), wire)
        parts = pltpu.VMEM((some, DH, DH), wire)
        total = pltpu.VMEM((rows, features), jnp.float32)
        many = pltpu.SemaphoreType.DMA((steps,))
        few = pltpu.SemaphoreType.DMA((some,))
        shape = jax.ShapeDtypeStruct((rows, features), jnp.bfloat16)
        inside = pltpu.MemorySpace.VMEM((rows, features), jnp.bfloat16)
        key_grad, value_grad = pl.pallas_call(
            functools.partial(kernel, ctx_count, heads, loose),
            out_shape=(inside, inside),
            in_specs=[pl.BlockSpec(memory_space=pltpu.SMEM), in_vmem] + [anywhere] * 4,
            out_specs=(in_vmem, in_vmem),
            scratch_shapes=[wide] * 4 + [
                pltpu.VMEM((rows // 2, features), jnp.bfloat16),
                pltpu.VMEM((owned, DH, rows), jnp.bfloat16)] + [small] * 5 + [
                pltpu.VMEM((steps, DH, DH), jnp.float32)] + [states] * 6 + [parts] * 4 + [
                pltpu.VMEM((owned + SKIPPED, DH, DH), jnp.bfloat16)] * 3 + [total] * 2 + [
                pltpu.VMEM((rows, rows), jnp.float32)] + [
                pltpu.SemaphoreType.DMA((5,)), pltpu.SemaphoreType.DMA((2, owned // 2 + 2)),
                pltpu.SemaphoreType.DMA((2,))] + [many] * 8 + [few] * 4 + [pltpu.SemaphoreType.REGULAR],
            compiler_params=pltpu.CompilerParams(
                collective_id=0, has_side_effects=True, vmem_limit_bytes=62 << 20),
        )(doc_ids, log_decay.T, queries, key_rows, value_rows, out_grad)
        return tuple(pl.pallas_call(
            handover,
            out_shape=(shape, shape),
            in_specs=[in_vmem] * 2,
            out_specs=(anywhere, anywhere),
            scratch_shapes=[pltpu.SemaphoreType.DMA((2, 4))],
            compiler_params=pltpu.CompilerParams(vmem_limit_bytes=16 << 20),
        )(key_grad, value_grad))

    placed = (
        P(("group", "ctx"), "tp"),
        P(("group", "ctx"), "tp"),
        P(("group", "ctx"), "tp"),
        P(("group", "ctx", "tp"), None),
        P(("group", "ctx"), "tp"),
        P("group"),
    )
    return jax.shard_map(
        per_device,
        mesh=mesh,
        in_specs=placed,
        out_specs=(P(("group", "ctx"), "tp"), P(("group", "ctx"), "tp")),
        check_vma=False,
    )
```
